32 devices in a mesh: tm: 8 (over y, x, core), stream: 4 (over z).
Axes of the slice: x: 2, y: 2, z: 4, core: 2. Of those that a mesh axis runs over, the one named last changes fastest.
Arguments:
- tokens: bfloat16 [4096, 2048], P(('tm', 'stream')), may hold values from -6 to 6
- w_query: bfloat16 [2048, 2048], P('stream'), may hold values from -0.125 to 0.125
- w_key: bfloat16 [2048, 2048], P('stream'), may hold values from -0.125 to 0.125
- w_value: bfloat16 [2048, 2048], P('stream'), may hold values from -0.125 to 0.125
- decay_proj: bfloat16 [2048, 16], P('stream'), may hold values from -0.125 to 0.125
- beta_proj: bfloat16 [2048, 16], P('stream'), may hold values from -0.125 to 0.125
- decay_rate: float32 [16], replicated, may hold values from 0.00024414062 to 0.1
- beta_bias: float32 [16], replicated, may hold values from -7 to 0
- norm_gain: float32 [128], replicated, may hold values from 0.5 to 1.5
Outputs:
- mixed: bfloat16 [4096, 2048], P(('tm', 'stream'))
The draws below stay inside these ranges and needn't reach their ends.
All inputs are finite; a program needn't handle non-finite values.
Results may differ from the reference program's by a relative error of at most 0.0073.
Values may be sent and summed in bfloat16 or wider, within the bound.
A program may use at most 128 MiB of HBM per device.

```python
import math
import jax
import jax.numpy as jnp
from jax import lax

D = 2048
HEADS = 16
DK = 128
DV = 128
GROUP = 256
TOKENS = 4096


def steps_of(rng, dims, split, smallest, largest):
    def one(axis_at, parts):
        heights = jax.random.uniform(jax.random.fold_in(jax.random.fold_in(rng, 6), axis_at), (parts,), jnp.float32, smallest / len(split), largest / len(split))
        return jnp.repeat(jnp.exp(heights), dims[axis_at] // parts).reshape((-1,) + (1,) * (len(dims) - axis_at - 1))

    loudness = one(*split[0])
    for cut in split[1:]:
        loudness = loudness * one(*cut)
    return loudness


def centred(own_key, dims, deviation, limit, cuts=(), held_as=jnp.bfloat16):
    entries = jax.random.normal(own_key, dims, jnp.float32) * deviation
    if len(cuts) > 0:
        entries = steps_of(own_key, dims, cuts, -0.22, 0.18) * entries
    return jnp.clip(entries, min=-limit, max=limit).astype(held_as)


def setup_inputs(seed: int = 0) -> dict:
    key_list = jax.random.split(jax.random.key(seed), 10)
    tokens = centred(key_list[0], (TOKENS, D), 1.0, 6.0, ((0, 32),))
    w_query = centred(key_list[1], (D, HEADS * DK), D ** -0.5, 0.125, ((0, 4),))
    w_key = centred(key_list[2], (D, HEADS * DK), D ** -0.5, 0.125, ((0, 4),))
    w_value = centred(key_list[3], (D, HEADS * DV), D ** -0.5, 0.125, ((0, 4),))
    decay_proj = centred(key_list[4], (D, HEADS), D ** -0.5, 0.125, ((0, 4),))
    beta_proj = centred(key_list[5], (D, HEADS), D ** -0.5, 0.125, ((0, 4),))
    decay_rate = jnp.clip(jnp.exp(jax.random.uniform(key_list[6], (HEADS,), jnp.float32, math.log(0.00024414062), math.log(0.1))), 0.00024414062, 0.1)
    beta_bias = jnp.clip(jax.random.uniform(key_list[7], (HEADS,), jnp.float32, -7.0, 0.0), -7.0, 0.0)
    norm_gain = jnp.clip(1.0 + 0.1 * jax.random.normal(key_list[8], (DV,), jnp.float32), 0.5, 1.5)
    return {"tokens": tokens, "w_query": w_query, "w_key": w_key, "w_value": w_value, "decay_proj": decay_proj, "beta_proj": beta_proj, "decay_rate": decay_rate, "beta_bias": beta_bias, "norm_gain": norm_gain}


highest_precision = lax.Precision.HIGHEST

def narrowed(value):
    return lax.optimization_barrier(value.astype(jnp.bfloat16)).astype(jnp.float32)

def reference(tokens, w_query, w_key, w_value, decay_proj, beta_proj, decay_rate, beta_bias, norm_gain):
    num_blocks = TOKENS // GROUP
    query_mat = w_query.astype(jnp.float32)
    key_mat = w_key.astype(jnp.float32)
    value_mat = w_value.astype(jnp.float32)
    decay_mat_w = decay_proj.astype(jnp.float32)
    beta_mat_w = beta_proj.astype(jnp.float32)
    blocks = tokens.reshape(num_blocks, GROUP, D)
    positions = jnp.arange(GROUP)
    strict = positions[:, None] > positions[None, :]
    inclusive_mask = positions[:, None] >= positions[None, :]
    identity = jnp.eye(GROUP, dtype=jnp.float32)

    def advance(state, block_rows):
        inputs = block_rows.astype(jnp.float32)
        raw_query = jnp.dot(inputs, query_mat, precision=highest_precision).reshape(GROUP, HEADS, DK)
        raw_key = jnp.dot(inputs, key_mat, precision=highest_precision).reshape(GROUP, HEADS, DK)
        queries = narrowed(raw_query * lax.rsqrt(lax.optimization_barrier(jnp.sum(raw_query * raw_query, -1, keepdims=True)) + 1e-06) * DK ** (-0.5))
        key_rows = narrowed(raw_key * lax.rsqrt(lax.optimization_barrier(jnp.sum(raw_key * raw_key, -1, keepdims=True)) + 1e-06))
        values = narrowed(jnp.dot(inputs, value_mat, precision=highest_precision)).reshape(GROUP, HEADS, DV)
        log_decay = narrowed(-decay_rate * jax.nn.softplus(jnp.dot(inputs, decay_mat_w, precision=highest_precision)))
        strength = narrowed(jax.nn.sigmoid(jnp.dot(inputs, beta_mat_w, precision=highest_precision) + beta_bias))
        cumulative = jnp.cumsum(log_decay, axis=0).T
        growth = jnp.exp(cumulative)
        last_log = cumulative[:, -1:]
        tail = jnp.exp(last_log - cumulative)
        strength_t = strength.T
        query_per_head = queries.transpose(1, 0, 2)
        key_per_head = key_rows.transpose(1, 0, 2)
        value_h = values.transpose(1, 0, 2)
        key_products = jnp.einsum('rxz,rfz->rxf', key_per_head, key_per_head, precision=highest_precision)
        spread = cumulative[:, :, None] - cumulative[:, None, :]
        decay_matrix = jnp.exp(jnp.where(inclusive_mask, spread, 0.0))
        lower = jnp.where(strict, strength_t[:, :, None] * decay_matrix * key_products, 0.0) + identity
        right_side = jnp.concatenate([(strength_t * growth)[..., None] * key_per_head, strength_t[..., None] * value_h], -1)
        solved = jax.scipy.linalg.solve_triangular(lower, right_side, lower=True, unit_diagonal=True)
        weights_w = solved[..., :DK]
        updates = solved[..., DK:]
        key_tail = tail[..., None] * key_per_head
        attention_scores = jnp.where(inclusive_mask, jnp.einsum('rxz,rfz->rxf', query_per_head, key_per_head, precision=highest_precision) * decay_matrix, 0.0)
        query_grown = growth[..., None] * query_per_head
        fresh = updates - jnp.einsum('hcd,hed->hce', weights_w, state, precision=highest_precision)
        read = jnp.einsum('hcd,hed->hce', query_grown, state, precision=highest_precision) + jnp.einsum('hcm,hme->hce', attention_scores, fresh, precision=highest_precision)
        new_state = jnp.exp(last_log)[..., None] * state + jnp.einsum('hce,hcd->hed', fresh, key_tail, precision=highest_precision)
        readout = narrowed(read).transpose(1, 0, 2)
        normed = readout * lax.rsqrt(lax.optimization_barrier(jnp.mean(readout * readout, -1, keepdims=True)) + 1e-06) * norm_gain
        return (new_state, normed.reshape(GROUP, HEADS * DV).astype(jnp.bfloat16))
    start = jnp.zeros((HEADS, DV, DK), jnp.float32)
    final_state, outputs = lax.scan(advance, start, blocks)
    return outputs.reshape(TOKENS, HEADS * DV)
```

```python
import functools

import jax
import jax.numpy as jnp
from jax import lax
from jax.experimental import pallas as pl
from jax.experimental.pallas import tpu as pltpu
from jax.sharding import PartitionSpec as P

HEADS = 16
DK = 128
DV = 128
CHUNK = 128
WIDTH = 2 * DK + DV
PIECES = 4
EARLY = 2
F32 = jnp.float32
BF16 = jnp.bfloat16


def halves(a):
    high = a.astype(BF16)
    return high, (a - high.astype(F32)).astype(BF16)


def contract(a, b, dims):
    return lax.dot_general(a, b, dims, preferred_element_type=F32)


def dot3(a, b, ca, cb, batch=0):
    ah, al = halves(a)
    bh, bl = halves(b)
    free = batch + (cb - batch + 1) % 2
    lead = tuple(range(batch))
    wide = jnp.concatenate([bh, bl], free)
    both = contract(
        jnp.concatenate([ah, al], ca),
        jnp.concatenate([wide, wide], cb),
        (((ca,), (cb,)), (lead, lead)),
    )
    half = both.shape[-1] // 2
    return both[..., :half] + both[..., half:]


def dot2(a, b, ca, cb):
    ah, al = halves(a)
    return contract(
        jnp.concatenate([ah, al], ca), jnp.concatenate([b, b], cb), (((ca,), (cb,)), ((), ()))
    )


def around(count):
    return sorted(range(1, count), key=lambda i: min(i, count - i))


def layer_kernel(
    streams,
    places,
    heads,
    senders,
    tok_ref,
    wq_ref,
    wk_ref,
    wv_ref,
    dec_ref,
    bet_ref,
    rate_ref,
    bias_ref,
    gain_ref,
    out_ref,
    x_ref,
    full,
    stage,
    gates,
    cum,
    cum_row,
    beta,
    read_ref,
    query_ref,
    own_map,
    sent_map,
    sib_map,
    total,
    got,
    prev,
    mixed,
    load_sem,
    own_sem,
    gate_load,
    tok_load,
    gate_send,
    gate_recv,
    gate_pass,
    gate_sib,
    right_sem,
    left_sem,
    tok_recv,
    cross_send,
    cross_recv,
    plane_send,
    pass_send,
    plane_recv,
    pair_send,
    pair_recv,
    chip_send,
    chip_recv,
    out_send,
    out_recv,
    out_own,
):
    t = lax.axis_index("tm")
    z = lax.axis_index("stream")
    chips = places // 2
    chip = t // 2
    core = t % 2
    sibling = chip * 2 + 1 - core
    depth = wq_ref.shape[0]
    share = depth // senders
    stride = places // senders
    step = max(stride // 2, 1)
    paired = stride == 1
    origins = senders // 2 if paired else senders
    base = chip // step * step
    local = tok_ref.shape[0]
    part = local // PIECES
    rows = streams * local
    chunks = rows // CHUNK
    near = around(streams)

    def remote(src, dst, send, recv, device):
        return pltpu.make_async_remote_copy(
            src_ref=src,
            dst_ref=dst,
            send_sem=send,
            recv_sem=recv,
            device_id=device,
            device_id_type=pl.DeviceIdType.MESH,
        )

    def only(cond, body):
        if cond is True:
            body()
        elif cond is not False:
            pl.when(cond)(body)

    is_sender = True if paired else (t % stride == 0)
    active = True if paired else (core == 0)
    mine = t // stride

    def slot(i):
        at = lax.rem(base + i * step, chips)
        return at, (2 * at + core if paired else at // step)

    weights = (wq_ref, wk_ref, wv_ref)

    own_gates = [
        pltpu.make_async_copy(dec_ref, gates.at[0, z], gate_load.at[0]),
        pltpu.make_async_copy(bet_ref, gates.at[1, z], gate_load.at[1]),
    ]
    for copy in own_gates:
        copy.start()

    def load_stage():
        for h in range(heads):
            for i in near:
                dest = lax.rem(z + i, streams)
                for j, ref in enumerate(weights):
                    cols = pl.ds(pl.multiple_of((dest * heads + h) * DK, DK), DK)
                    at = pl.ds(pl.multiple_of(mine * share, share), share)
                    pltpu.make_async_copy(
                        ref.at[at, cols],
                        stage.at[dest, h, :, pl.ds(j * DK, DK)],
                        load_sem.at[dest, h],
                    ).start()

    only(is_sender, load_stage)
    own_tok = pltpu.make_async_copy(tok_ref, x_ref.at[z], tok_load.at[0])
    own_tok.start()
    for h in range(heads):
        for j, ref in enumerate(weights):
            cols = pl.ds(pl.multiple_of((z * heads + h) * DK, DK), DK)
            pltpu.make_async_copy(
                ref.at[:, cols], full.at[h, z, :, pl.ds(j * DK, DK)], own_sem.at[h]
            ).start()

    others = [lax.rem(chip + i, chips) * 2 + core for i in range(1, chips)]
    peers = [(t, lax.rem(z + i, streams)) for i in near]
    peers += [(sibling, z)] + [(o, z) for o in others]
    barrier = pltpu.get_barrier_semaphore()
    for peer in peers:
        pl.semaphore_signal(
            barrier, inc=1, device_id=peer, device_id_type=pl.DeviceIdType.MESH
        )
    pl.semaphore_wait(barrier, len(peers))

    def line(s, p, right, first):
        at = pl.ds(p * part, part)
        src = tok_ref.at[at] if first else x_ref.at[s, at]
        send = (right_sem if right else left_sem).at[s, p]
        return remote(
            src, x_ref.at[s, at], send, tok_recv.at[s, p], (t, z + 1 if right else z - 1)
        )

    def gate_out(i):
        dest = lax.rem(z + i, streams)
        here = gates.at[core, z]
        return remote(here, here, gate_send.at[dest], gate_recv.at[z], (t, dest))

    def gate_in(i):
        s = lax.rem(z + i, streams)
        here = gates.at[core, s]
        return remote(here, here, gate_send.at[s], gate_recv.at[s], (t, s))

    def gate_on(i):
        s = lax.rem(z + i, streams)
        here = gates.at[core, s]
        return remote(here, here, gate_pass.at[s], gate_sib.at[s], (sibling, z))

    def gate_landed(i):
        s = lax.rem(z + i, streams)
        here = gates.at[1 - core, s]
        return remote(here, here, gate_pass.at[s], gate_sib.at[s], (sibling, z))

    def rows_of(k):
        return pl.ds(pl.multiple_of(k * share, share), share)

    def cross(u, i):
        dest = lax.rem(z + i, streams)
        return remote(
            stage.at[dest, u],
            full.at[u, z, rows_of(mine)],
            cross_send.at[dest, u],
            cross_recv.at[z, u],
            (t, dest),
        )

    def crossed(u, i):
        s = lax.rem(z + i, streams)
        return remote(
            stage.at[s, u],
            full.at[u, s, rows_of(mine)],
            cross_send.at[s, u],
            cross_recv.at[s, u],
            (t, s),
        )

    def plane(u, i, s):
        to = sibling if i == 0 else others[i - 1]
        here = full.at[u, s, rows_of(mine)]
        return remote(
            here, here, plane_send.at[i, s, u], plane_recv.at[mine, s, u], (to, z)
        )

    def relay(u, i, s):
        k = slot(i)[1]
        here = full.at[u, s, rows_of(k)]
        return remote(here, here, pass_send.at[i, s, u], plane_recv.at[k, s, u], (sibling, z))

    def landed(u, k, s):
        here = full.at[u, s, rows_of(k)]
        return remote(here, here, plane_send.at[0, s, u], plane_recv.at[k, s, u], (sibling, z))

    def issue(u):
        def body():
            for i in near:
                dest = lax.rem(z + i, streams)
                pltpu.make_async_copy(
                    stage.at[dest, u], stage.at[dest, u], load_sem.at[dest, u]
                ).wait()
                cross(u, i).start()

        only(is_sender, body)

    def spread(u):
        def body():
            for i in near:
                s = lax.rem(z + i, streams)
                crossed(u, i).wait_recv()
                for j in range(1, chips):
                    plane(u, j, s).start()
                plane(u, 0, s).start()

        only(is_sender, body)

    def pass_on(u):
        for i in range(origins):
            at, k = slot(i)
            if i == 0:
                if paired:
                    continue
                cond = active & (chip != base)
            else:
                cond = active

            def body(i=i, k=k):
                for n in near:
                    s = lax.rem(z + n, streams)
                    landed(u, k, s).wait_recv()
                    relay(u, i, s).start()

            only(cond, body)

    def arrived(u):
        def body():
            for k in range(origins):
                origin = 2 * k + 1 - core if paired else k
                for n in near:
                    landed(u, origin, lax.rem(z + n, streams)).wait_recv()

        only(True if paired else core == 1, body)
        pltpu.make_async_copy(full.at[u, z], full.at[u, z], own_sem.at[u]).wait()

    def token_step(k, p):
        @pl.when(z >= k)
        def _():
            line(z - k, p, True, False).wait_recv()

            @pl.when(z < streams - 1)
            def _():
                line(z - k, p, True, False).start()

        @pl.when(z + k < streams)
        def _():
            line(z + k, p, False, False).wait_recv()

            @pl.when(z > 0)
            def _():
                line(z + k, p, False, False).start()

    for copy in own_gates:
        copy.wait()
    for i in near:
        gate_out(i).start()
    for p in range(PIECES):

        @pl.when(z < streams - 1)
        def _():
            line(z, p, True, True).start()

        @pl.when(z > 0)
        def _():
            line(z, p, False, True).start()

    early = range(min(EARLY, heads))
    late = range(min(EARLY, heads), heads)
    for u in early:
        issue(u)
    for k in range(1, streams):
        for p in range(PIECES):
            token_step(k, p)
        if k == 1:
            for i in near:
                gate_in(i).wait_recv()
                gate_on(i).start()
            for u in early:
                spread(u)
        if k == max(streams - 2, 1):
            for u in late:
                issue(u)
            for u in early:
                pass_on(u)
    own_tok.wait()
    for i in near:
        gate_landed(i).wait_recv()

    row_at = lax.broadcasted_iota(jnp.int32, (CHUNK, CHUNK), 0)
    col_at = lax.broadcasted_iota(jnp.int32, (CHUNK, CHUNK), 1)
    low = row_at >= col_at
    strict = row_at > col_at
    eye = jnp.where(row_at == col_at, 1.0, 0.0)
    lower_ones = jnp.where(low, 1.0, 0.0).astype(BF16)

    def logits(which):
        sums = None
        for s in range(streams):
            x = x_ref[:, :, pl.ds(s * depth, depth)].reshape(rows, depth)
            term = contract(x, gates[which, s], (((1,), (1,)), ((), ())))
            sums = term if sums is None else sums + term
        return sums

    first = logits(0)
    soft = jnp.maximum(first, 0.0) + jnp.log1p(jnp.exp(-jnp.abs(first)))
    decay = (-rate_ref[...] * soft).astype(BF16)
    beta[...] = (
        (1.0 / (1.0 + jnp.exp(-(logits(1) + bias_ref[...])))).astype(BF16).astype(F32)
    ).reshape(chunks, CHUNK, HEADS)
    for c in range(chunks):
        sums = contract(
            lower_ones, decay[c * CHUNK : (c + 1) * CHUNK], (((1,), (0,)), ((), ()))
        )
        cum[c] = sums
        cum_row[c] = sums.T

    lane = lax.broadcasted_iota(jnp.int32, (chunks, CHUNK, HEADS), 2)

    def pair_copy(h):
        return remote(
            sent_map.at[h], sib_map.at[h], pair_send.at[h], pair_recv.at[h], (sibling, z)
        )

    def to_chip(h, source, dest):
        src, dst = total.at[h], got.at[source, h]
        if source == 0:
            src, dst = total.at[h, pl.ds(DK, DV)], got.at[0, h, pl.ds(DK, DV)]
        return remote(
            src, dst, chip_send.at[dest, h], chip_recv.at[source, h], (dest * 2 + core, z)
        )

    def compute(h):
        x = x_ref[...].reshape(rows, x_ref.shape[2])
        w = full[h].reshape(streams * depth, WIDTH)
        raw = contract(x, w, (((1,), (0,)), ((), ())))
        raw_q = raw[:, :DK]
        raw_k = raw[:, DK : 2 * DK]
        q = (
            raw_q * lax.rsqrt(jnp.sum(raw_q * raw_q, -1, keepdims=True) + 1e-06) * DK ** (-0.5)
        ).astype(BF16)
        k = (raw_k * lax.rsqrt(jnp.sum(raw_k * raw_k, -1, keepdims=True) + 1e-06)).astype(BF16)
        v = raw[:, 2 * DK :].astype(BF16)
        q = q.reshape(chunks, CHUNK, DK)
        k = k.reshape(chunks, CHUNK, DK)
        v = v.reshape(chunks, CHUNK, DV).astype(F32)
        head = z * heads + h
        g = jnp.sum(jnp.where(lane == head, cum[...], 0.0), -1, keepdims=True)
        b = jnp.sum(jnp.where(lane == head, beta[...], 0.0), -1, keepdims=True)
        g_row = cum_row[:, pl.ds(head, 1), :]
        g_last = g[:, CHUNK - 1 :, :]
        growth = jnp.exp(g)
        tail = jnp.exp(g_last - g)
        whole = jnp.exp(g_last)

        pair = contract(jnp.concatenate([k, q], 1), k, (((2,), (2,)), ((0,), (0,))))
        spread_ = jnp.exp(jnp.where(low[None], g - g_row, 0.0))
        lmat = jnp.where(strict[None], b * spread_ * pair[:, :CHUNK], 0.0)
        mmat = jnp.where(low[None], spread_ * pair[:, CHUNK:], 0.0)

        inverse = None
        size = 1
        while size < CHUNK:
            inside = (row_at // (2 * size) == col_at // (2 * size)) & (
                row_at // size != col_at // size
            )
            off = jnp.where(inside[None], lmat, 0.0)
            if inverse is None:
                inverse = eye[None] - off
            else:
                inverse = inverse - dot3(inverse, dot3(off, inverse, 2, 1, 1), 2, 1, 1)
            size *= 2

        kf = k.astype(F32)
        right = jnp.concatenate([(b * growth) * kf, b * v], 2)
        wu = dot3(inverse, right, 2, 1, 1)
        key_tail = tail * kf
        jumps = dot3(jnp.swapaxes(wu, 1, 2), key_tail, 2, 1, 1)
        step_map = whole * eye[None] - jumps[:, :DK]
        carry = jnp.concatenate([step_map[0], jumps[0, DK:]], 0)
        carries = [carry]
        for c in range(1, chunks):
            moved = dot3(carry, step_map[c], 1, 0)
            carry = jnp.concatenate([moved[:DK], moved[DK:] + jumps[c, DK:]], 0)
            carries.append(carry)
        own_map[h] = carry
        sent_map[h] = carry.astype(BF16)
        pair_copy(h).start()

        mwu = dot3(mmat, wu, 2, 1, 1)
        moved = growth * q.astype(F32) - mwu[:, :, :DK]
        for c in range(chunks):
            if c == 0:
                query_ref[h, c] = moved[c]
                read_ref[h, c] = mwu[c, :, DK:]
                continue
            both = dot3(moved[c], carries[c - 1], 1, 1)
            query_ref[h, c] = both[:, :DK]
            read_ref[h, c] = mwu[c, :, DK:] + both[:, DK:]

    def join(h):
        pair_copy(h).wait_recv()

        @pl.when(chip < chips - 1)
        def _():
            own = own_map[h]
            other = sib_map[h].astype(F32)
            before = jnp.where(core == 0, own, other)
            after = jnp.where(core == 0, other, own)
            both = dot3(before, after[:DK], 1, 0)
            total[h, :DK] = both[:DK].astype(BF16)
            total[h, DK:] = (both[DK:] + after[DK:]).astype(BF16)

        for source in range(chips - 1):

            @pl.when(chip == source)
            def _():
                for dest in range(chips - 1, source, -1):
                    to_chip(h, source, dest).start()

    def enter(h):
        @pl.when(chip == 0)
        def _():
            prev[h] = jnp.zeros((DV, DK), F32)

        for source in range(chips - 1):

            @pl.when(chip > source)
            def _():
                to_chip(h, source, chip).wait_recv()
                if source == 0:
                    prev[h] = got[0, h, DK:].astype(F32)
                else:
                    prev[h] = dot2(prev[h], got[source, h, :DK], 1, 0) + got[
                        source, h, DK:
                    ].astype(F32)

        @pl.when(core == 1)
        def _():
            prev[h] = dot2(prev[h], sib_map[h, :DK], 1, 0) + sib_map[h, DK:].astype(F32)

    def place(h, source):
        return out_ref.at[:, pl.ds(pl.multiple_of((source * heads + h) * DV, DV), DV)]

    def outgoing(h, i):
        dest = lax.rem(z + i, streams)
        return remote(
            mixed.at[h, dest], place(h, z), out_send.at[dest, h], out_recv.at[z, h], (t, dest)
        )

    def incoming(h, i):
        source = lax.rem(z + i, streams)
        return remote(
            mixed.at[h, source],
            place(h, source),
            out_send.at[source, h],
            out_recv.at[source, h],
            (t, source),
        )

    def own_out(h):
        return pltpu.make_async_copy(mixed.at[h, z], place(h, z), out_own.at[h])

    far = list(reversed(near))
    per = local // CHUNK

    def finish(h):
        state = prev[h]
        for i in far + [0]:
            dest = lax.rem(z + i, streams)
            for c in range(per):
                at = dest * per + c
                read = read_ref[h, at] + dot3(query_ref[h, at], state, 1, 1)
                readout = read.astype(BF16).astype(F32)
                scale = lax.rsqrt(jnp.mean(readout * readout, -1, keepdims=True) + 1e-06)
                mixed[h, dest, c * CHUNK : (c + 1) * CHUNK] = (
                    readout * scale * gain_ref[...]
                ).astype(BF16)
            if i == 0:
                own_out(h).start()
            else:
                outgoing(h, i).start()

    stages = (join, enter, finish)
    for h in range(heads + len(stages)):
        if h < heads:
            if h in late:
                pass_on(h)
            if h + 1 in late:
                spread(h + 1)
            arrived(h)
            compute(h)
        for n, run in enumerate(stages):
            at = h - n if h >= heads else h - n - 1
            if h >= heads:
                at = h - n - 1
            if 0 <= at < heads:
                run(at)

    for h in range(heads):
        own_out(h).wait()
        for i in far:
            incoming(h, i).wait_recv()
    for h in range(heads):
        for i in far:
            outgoing(h, i).wait_send()
        pair_copy(h).wait_send()
        for source in range(chips - 1):

            @pl.when(chip == source)
            def _():
                for dest in range(chips - 1, source, -1):
                    to_chip(h, source, dest).wait_send()

    for u in range(heads):

        def sent():
            for n in near:
                cross(u, n).wait_send()
                s = lax.rem(z + n, streams)
                for j in range(chips):
                    plane(u, j, s).wait_send()

        only(is_sender, sent)
        for i in range(origins):
            if i == 0:
                if paired:
                    continue
                cond = active & (chip != base)
            else:
                cond = active

            def passed():
                for n in near:
                    relay(u, i, lax.rem(z + n, streams)).wait_send()

            only(cond, passed)
    for i in near:
        gate_out(i).wait_send()
        gate_on(i).wait_send()
    for k in range(streams):
        for p in range(PIECES):

            @pl.when((z >= k) & (z < streams - 1))
            def _():
                line(z - k, p, True, k == 0).wait_send()

            @pl.when((z + k < streams) & (z > 0))
            def _():
                line(z + k, p, False, k == 0).wait_send()


def shards(
    tokens, w_query, w_key, w_value, decay_proj, beta_proj, decay_rate, beta_bias, norm_gain
):
    streams = lax.axis_size("stream")
    places = lax.axis_size("tm")
    heads = HEADS // streams
    depth = w_query.shape[0]
    senders = min(places, depth // 16)
    share = depth // senders
    local, features = tokens.shape
    rows = streams * local
    chunks = rows // CHUNK
    chips = places // 2
    any_space = pl.BlockSpec(memory_space=pl.ANY)
    vmem = pl.BlockSpec(memory_space=pltpu.VMEM)
    dma = pltpu.SemaphoreType.DMA
    return pl.pallas_call(
        functools.partial(layer_kernel, streams, places, heads, senders),
        out_shape=jax.ShapeDtypeStruct((local, HEADS * DV), BF16),
        in_specs=[any_space] * 6 + [vmem] * 3,
        out_specs=any_space,
        scratch_shapes=[
            pltpu.VMEM((streams, local, features), BF16),
            pltpu.VMEM((heads, streams, depth, WIDTH), BF16),
            pltpu.VMEM((streams, heads, share, WIDTH), BF16),
            pltpu.VMEM((2, streams, HEADS, depth), BF16),
            pltpu.VMEM((chunks, CHUNK, HEADS), F32),
            pltpu.VMEM((chunks, HEADS, CHUNK), F32),
            pltpu.VMEM((chunks, CHUNK, HEADS), F32),
            pltpu.VMEM((heads, chunks, CHUNK, DV), F32),
            pltpu.VMEM((heads, chunks, CHUNK, DK), F32),
            pltpu.VMEM((heads, DK + DV, DK), F32),
            pltpu.VMEM((heads, DK + DV, DK), BF16),
            pltpu.VMEM((heads, DK + DV, DK), BF16),
            pltpu.VMEM((heads, DK + DV, DK), BF16),
            pltpu.VMEM((chips, heads, DK + DV, DK), BF16),
            pltpu.VMEM((heads, DV, DK), F32),
            pltpu.VMEM((heads, streams, local, DV), BF16),
            dma((streams, heads)),
            dma((heads,)),
            dma((2,)),
            dma((1,)),
            dma((streams,)),
            dma((streams,)),
            dma((streams,)),
            dma((streams,)),
            dma((streams, PIECES)),
            dma((streams, PIECES)),
            dma((streams, PIECES)),
            dma((streams, heads)),
            dma((streams, heads)),
            dma((chips, streams, heads)),
            dma((max(senders, chips), streams, heads)),
            dma((senders, streams, heads)),
            dma((heads,)),
            dma((heads,)),
            dma((chips, heads)),
            dma((chips, heads)),
            dma((streams, heads)),
            dma((streams, heads)),
            dma((heads,)),
        ],
        compiler_params=pltpu.CompilerParams(collective_id=0, has_side_effects=True),
    )(
        tokens,
        w_query,
        w_key,
        w_value,
        decay_proj.T,
        beta_proj.T,
        decay_rate[None],
        beta_bias[None],
        norm_gain[None],
    )


def solution(mesh):
    return jax.shard_map(
        shards,
        mesh=mesh,
        in_specs=(
            P(("tm", "stream"), None),
            P("stream", None),
            P("stream", None),
            P("stream", None),
            P("stream", None),
            P("stream", None),
            P(),
            P(),
            P(),
        ),
        out_specs=P(("tm", "stream"), None),
        check_vma=False,
    )
```

```python
import functools

import jax
import jax.numpy as jnp
from jax import lax
from jax.experimental import pallas as pl
from jax.experimental.pallas import tpu as pltpu
from jax.sharding import PartitionSpec as P

HEADS = 16
DK = 128
DV = 128
CHUNK = 128
PIECES = 4
GROUPS = 2
F32 = jnp.float32
BF16 = jnp.bfloat16


def halves(a):
    high = a.astype(BF16)
    return high, (a - high.astype(F32)).astype(BF16)


def contract(a, b, dims):
    return lax.dot_general(a, b, dims, preferred_element_type=F32)


def dot3(a, b, ca, cb, batch=0):
    ah, al = halves(a)
    bh, bl = halves(b)
    free = batch + (cb - batch + 1) % 2
    lead = tuple(range(batch))
    wide = jnp.concatenate([bh, bl], free)
    both = contract(
        jnp.concatenate([ah, al], ca),
        jnp.concatenate([wide, wide], cb),
        (((ca,), (cb,)), (lead, lead)),
    )
    half = both.shape[-1] // 2
    return both[..., :half] + both[..., half:]


def dot2(a, b, ca, cb):
    ah, al = halves(a)
    return contract(
        jnp.concatenate([ah, al], ca), jnp.concatenate([b, b], cb), (((ca,), (cb,)), ((), ()))
    )


def around(count):
    return sorted(range(1, count), key=lambda i: min(i, count - i))


def layer_kernel(
    streams,
    places,
    heads,
    senders,
    tok_ref,
    wq_ref,
    wk_ref,
    wv_ref,
    dec_ref,
    bet_ref,
    rate_ref,
    bias_ref,
    gain_ref,
    out_ref,
    x_ref,
    full,
    stage,
    gates,
    cum_row,
    step_ref,
    run_ref,
    read_ref,
    query_ref,
    sent_map,
    sib_map,
    total,
    got,
    prev,
    mixed,
    load_sem,
    own_sem,
    gate_load,
    tok_load,
    gate_send,
    gate_recv,
    gate_pass,
    gate_sib,
    right_sem,
    left_sem,
    tok_recv,
    cross_send,
    cross_recv,
    plane_send,
    plane_recv,
    pass_send,
    sib_recv,
    pair_send,
    pair_recv,
    chip_send,
    chip_recv,
    out_send,
    out_recv,
    out_own,
):
    t = lax.axis_index("tm")
    z = lax.axis_index("stream")
    chips = places // 2
    chip = t // 2
    core = t % 2
    sibling = chip * 2 + 1 - core
    depth = wq_ref.shape[0]
    share = depth // senders
    stride = places // senders
    step = max(stride // 2, 1)
    paired = stride == 1
    origins = senders // 2 if paired else senders
    base = chip // step * step
    local, features = tok_ref.shape
    part = local // PIECES
    near = around(streams)
    span = heads * DK
    groups = GROUPS if heads % GROUPS == 0 else 1
    each = heads // groups

    def remote(src, dst, send, recv, device):
        return pltpu.make_async_remote_copy(
            src_ref=src,
            dst_ref=dst,
            send_sem=send,
            recv_sem=recv,
            device_id=device,
            device_id_type=pl.DeviceIdType.MESH,
        )

    def drain(ref, sem):
        pltpu.make_async_copy(ref, ref, sem).wait()

    def only(cond, body):
        if cond is True:
            body()
        elif cond is not False:
            pl.when(cond)(body)

    is_sender = True if paired else (t % stride == 0)
    active = True if paired else (core == 0)
    mine = t // stride

    def slot(i):
        at = lax.rem(base + i * step, chips)
        return 2 * at + core if paired else at // step

    weights = (wq_ref, wk_ref, wv_ref)
    my_rows = pl.ds(pl.multiple_of(mine * share, share), share)

    def load_stage():
        for i in near:
            dest = lax.rem(z + i, streams)
            for j, ref in enumerate(weights):
                pltpu.make_async_copy(
                    ref.at[my_rows, pl.ds(pl.multiple_of(dest * span, span), span)],
                    stage.at[dest, :, pl.ds(j * span, span)],
                    load_sem.at[dest],
                ).start()

    only(is_sender, load_stage)
    pltpu.make_async_copy(dec_ref, gates.at[0, z], gate_load.at[0]).start()
    pltpu.make_async_copy(bet_ref, gates.at[1, z], gate_load.at[0]).start()
    own_tok = pltpu.make_async_copy(tok_ref, x_ref.at[z], tok_load.at[0])
    own_tok.start()
    for j, ref in enumerate(weights):
        pltpu.make_async_copy(
            ref.at[:, pl.ds(pl.multiple_of(z * span, span), span)],
            full.at[z, :, pl.ds(j * span, span)],
            own_sem.at[0],
        ).start()

    others = [lax.rem(chip + i, chips) * 2 + core for i in range(1, chips)]
    peers = [(t, lax.rem(z + i, streams)) for i in near]
    peers += [(sibling, z)] + [(o, z) for o in others]
    barrier = pltpu.get_barrier_semaphore()
    for peer in peers:
        pl.semaphore_signal(
            barrier, inc=1, device_id=peer, device_id_type=pl.DeviceIdType.MESH
        )
    pl.semaphore_wait(barrier, len(peers))

    def rows_of(k):
        return pl.ds(pl.multiple_of(k * share, share), share)

    def line(s, p, right, first):
        at = pl.ds(p * part, part)
        src = tok_ref.at[at] if first else x_ref.at[s, at]
        send = (right_sem if right else left_sem).at[s]
        return remote(
            src, x_ref.at[s, at], send, tok_recv.at[s, p], (t, z + 1 if right else z - 1)
        )

    def gate_out(i):
        dest = lax.rem(z + i, streams)
        here = gates.at[core, z]
        return remote(here, here, gate_send.at[0], gate_recv.at[z], (t, dest))

    def gate_in(i):
        s = lax.rem(z + i, streams)
        here = gates.at[core, s]
        return remote(here, here, gate_send.at[0], gate_recv.at[s], (t, s))

    def gate_on(i):
        s = lax.rem(z + i, streams)
        here = gates.at[core, s]
        return remote(here, here, gate_pass.at[0], gate_sib.at[0], (sibling, z))

    def cross(i):
        dest = lax.rem(z + i, streams)
        return remote(
            stage.at[dest], full.at[z, rows_of(mine)], cross_send.at[0], cross_recv.at[z], (t, dest)
        )

    def crossed(i):
        s = lax.rem(z + i, streams)
        return remote(
            stage.at[s], full.at[s, rows_of(mine)], cross_send.at[0], cross_recv.at[s], (t, s)
        )

    def plane(i, s):
        here = full.at[s, rows_of(mine)]
        return remote(
            here, here, plane_send.at[i], plane_recv.at[mine, s], (others[i - 1], z)
        )

    def beside(k, s):
        here = full.at[s, rows_of(k)]
        return remote(here, here, pass_send.at[0], sib_recv.at[0], (sibling, z))

    def landed(k, s):
        here = full.at[s, rows_of(k)]
        return remote(here, here, plane_send.at[0], plane_recv.at[k, s], (others[0], z))

    def token_step(k, pieces):
        for p in pieces:

            @pl.when(z >= k)
            def _():
                line(z - k, p, True, False).wait_recv()

                @pl.when(z < streams - 1)
                def _():
                    line(z - k, p, True, False).start()

            @pl.when(z + k < streams)
            def _():
                line(z + k, p, False, False).wait_recv()

                @pl.when(z > 0)
                def _():
                    line(z + k, p, False, False).start()

    def send_shares():
        for i in near:
            drain(stage.at[lax.rem(z + i, streams)], load_sem.at[lax.rem(z + i, streams)])
            cross(i).start()

    only(is_sender, send_shares)
    drain(gates.at[:, z], gate_load.at[0])
    for i in near:
        gate_out(i).start()
    for p in range(PIECES):

        @pl.when(z < streams - 1)
        def _():
            line(z, p, True, True).start()

        @pl.when(z > 0)
        def _():
            line(z, p, False, True).start()

    def spread():
        for i in near:
            s = lax.rem(z + i, streams)
            crossed(i).wait_recv()
            for j in range(1, chips):
                plane(j, s).start()
            beside(mine, s).start()

    only(is_sender, spread)
    for i in near:
        gate_in(i).wait_recv()
        gate_on(i).start()

    def pass_on(i):
        if i == 0:
            if paired:
                return
            cond = active & (chip != base)
        else:
            cond = active
        k = slot(i)

        def body():
            for n in near:
                s = lax.rem(z + n, streams)
                landed(k, s).wait_recv()
                beside(k, s).start()

        only(cond, body)

    for p in range(PIECES):
        token_step(1, [p])
        for i in range(origins * p // PIECES, origins * (p + 1) // PIECES):
            pass_on(i)
    own_tok.wait()
    drain(full.at[z], own_sem.at[0])
    drain(gates.at[0, pl.ds(0, streams - 1)], gate_sib.at[0])
    only(
        True if paired else core == 1,
        lambda: drain(full.at[pl.ds(0, streams - 1), pl.ds(0, origins * share)], sib_recv.at[0]),
    )

    row_at = lax.broadcasted_iota(jnp.int32, (CHUNK, CHUNK), 0)
    col_at = lax.broadcasted_iota(jnp.int32, (CHUNK, CHUNK), 1)
    low = row_at >= col_at
    strict = row_at > col_at
    eye = jnp.where(row_at == col_at, 1.0, 0.0)
    lower_ones = jnp.where(low, 1.0, 0.0).astype(BF16)
    lane = lax.broadcasted_iota(jnp.int32, (CHUNK, HEADS), 1)

    def turn(n):
        fewer = jnp.minimum(z, streams - 1 - z)
        left = z * 2 >= streams
        both = n <= 2 * fewer
        k = jnp.where(both, (n + 1) // 2, n - fewer)
        leftward = jnp.where(both, jnp.where(left, n % 2 == 0, n % 2 == 1), left)
        at = jnp.where(leftward, z - k, z + k)
        return (z, None) if n == 0 else (at, leftward)

    def columns(a, first):
        picked = [
            jnp.sum(jnp.where(lane == z * heads + h, a, 0.0), -1, keepdims=True)
            for h in range(heads)
        ]
        return jnp.stack(picked)

    def split(a):
        return jnp.stack([a[:, h * DK : (h + 1) * DK] for h in range(heads)])

    def process(n):
        at, leftward = turn(n)
        x = x_ref[at]
        sums = None
        for s in range(streams):
            g2 = gates[:, s].reshape(2 * HEADS, depth)
            term = contract(x[:, s * depth : (s + 1) * depth], g2, (((1,), (1,)), ((), ())))
            sums = term if sums is None else sums + term
        first = sums[:, :HEADS]
        soft = jnp.maximum(first, 0.0) + jnp.log1p(jnp.exp(-jnp.abs(first)))
        decay = (-rate_ref[...] * soft).astype(BF16)
        beta = (1.0 / (1.0 + jnp.exp(-(sums[:, HEADS:] + bias_ref[...])))).astype(BF16).astype(F32)
        cum = contract(lower_ones, decay, (((1,), (0,)), ((), ())))
        cum_row[...] = cum.T
        g = columns(cum, 0)
        b = columns(beta, 0)
        g_row = jnp.stack([cum_row[pl.ds(z * heads + h, 1), :] for h in range(heads)])

        def project(j):
            w = full[:, :, j * span : (j + 1) * span].reshape(streams * depth, span)
            return split(contract(x, w, (((1,), (0,)), ((), ()))))

        raw_k = project(1)
        k = (raw_k * lax.rsqrt(jnp.sum(raw_k * raw_k, -1, keepdims=True) + 1e-06)).astype(BF16)
        raw_q = project(0)
        q = (
            raw_q * lax.rsqrt(jnp.sum(raw_q * raw_q, -1, keepdims=True) + 1e-06) * DK ** (-0.5)
        ).astype(BF16)
        v = project(2).astype(BF16).astype(F32)
        g_last = g[:, CHUNK - 1 :, :]
        growth = jnp.exp(g)
        tail = jnp.exp(g_last - g)
        whole = jnp.exp(g_last)

        pair = contract(jnp.concatenate([k, q], 1), k, (((2,), (2,)), ((0,), (0,))))
        spread_ = jnp.exp(jnp.where(low[None], g - g_row, 0.0))
        lmat = jnp.where(strict[None], b * spread_ * pair[:, :CHUNK], 0.0)
        mmat = jnp.where(low[None], spread_ * pair[:, CHUNK:], 0.0)

        inverse = None
        size = 1
        while size < CHUNK:
            inside = (row_at // (2 * size) == col_at // (2 * size)) & (
                row_at // size != col_at // size
            )
            off = jnp.where(inside[None], lmat, 0.0)
            if inverse is None:
                inverse = eye[None] - off
            else:
                inverse = inverse - dot3(inverse, dot3(off, inverse, 2, 1, 1), 2, 1, 1)
            size *= 2

        kf = k.astype(F32)
        right = jnp.concatenate([(b * growth) * kf, b * v], 2)
        wu = dot3(inverse, right, 2, 1, 1)
        jumps = dot3(jnp.swapaxes(wu, 1, 2), tail * kf, 2, 1, 1)
        step_map = jnp.concatenate([whole * eye[None] - jumps[:, :DK], jumps[:, DK:]], 1)
        step_ref[at] = step_map
        if n == 0:
            run = step_map
        else:
            run = run_ref[...]
            before = jnp.where(leftward, step_map, run)
            after = jnp.where(leftward, run, step_map)
            run = join_maps(before, after)
        if n < streams - 1:
            run_ref[...] = run
        else:
            sent_map[...] = run.astype(BF16)
            for gr in range(groups):
                pair_copy(gr).start()
            run_ref[...] = run
        mwu = dot3(mmat, wu, 2, 1, 1)
        query_ref[at] = growth * q.astype(F32) - mwu[:, :, :DK]
        read_ref[at] = mwu[:, :, DK:]

    def join_maps(before, after):
        both = dot3(before, after[:, :DK], 2, 1, 1)
        return jnp.concatenate([both[:, :DK], both[:, DK:] + after[:, DK:]], 1)

    def group(gr):
        return pl.ds(gr * each, each)

    def pair_copy(gr):
        return remote(
            sent_map.at[group(gr)],
            sib_map.at[group(gr)],
            pair_send.at[gr],
            pair_recv.at[gr],
            (sibling, z),
        )

    def to_chip(gr, source, dest):
        src, dst = total.at[group(gr)], got.at[source, group(gr)]
        if source == 0:
            src = total.at[group(gr), pl.ds(DK, DV)]
            dst = got.at[0, group(gr), pl.ds(DK, DV)]
        return remote(
            src, dst, chip_send.at[dest, gr], chip_recv.at[source, gr], (dest * 2 + core, z)
        )

    for n in range(streams):
        process(n)
        if n == 0 and streams > 2:
            token_step(2, range(PIECES // 2))
        elif n == 1 and streams > 2:
            token_step(2, range(PIECES // 2, PIECES))
        elif 2 <= n < streams - 1:
            token_step(n + 1, range(PIECES))

    def join(gr):
        pair_copy(gr).wait_recv()

        @pl.when(chip < chips - 1)
        def _():
            own = run_ref[gr * each : (gr + 1) * each]
            other = sib_map[gr * each : (gr + 1) * each].astype(F32)
            before = jnp.where(core == 0, own, other)
            after = jnp.where(core == 0, other, own)
            total[gr * each : (gr + 1) * each] = join_maps(before, after).astype(BF16)

        for source in range(chips - 1):

            @pl.when(chip == source)
            def _():
                for dest in range(chips - 1, source, -1):
                    to_chip(gr, source, dest).start()

    def prefixes():
        carry = step_ref[0]
        for c in range(1, streams):
            both = dot3(query_ref[c], carry, 2, 2, 1)
            query_ref[c] = both[:, :, :DK]
            read_ref[c] = read_ref[c] + both[:, :, DK:]
            if c < streams - 1:
                carry = join_maps(carry, step_ref[c])

    def enter(gr):
        hs = range(gr * each, (gr + 1) * each)

        @pl.when(chip == 0)
        def _():
            for h in hs:
                prev[h] = jnp.zeros((DV, DK), F32)

        for source in range(chips - 1):

            @pl.when(chip > source)
            def _():
                to_chip(gr, source, chip).wait_recv()
                for h in hs:
                    if source == 0:
                        prev[h] = got[0, h, DK:].astype(F32)
                    else:
                        prev[h] = dot2(prev[h], got[source, h, :DK], 1, 0) + got[
                            source, h, DK:
                        ].astype(F32)

        @pl.when(core == 1)
        def _():
            for h in hs:
                prev[h] = dot2(prev[h], sib_map[h, :DK], 1, 0) + sib_map[h, DK:].astype(F32)

    wide = each * DV

    def spot(gr, source):
        return out_ref.at[
            :, pl.ds(pl.multiple_of(source * span + gr * wide, wide), wide)
        ]

    def outgoing(gr, i):
        dest = lax.rem(z + i, streams)
        return remote(
            mixed.at[gr, dest], spot(gr, z), out_send.at[dest, gr], out_recv.at[z, gr], (t, dest)
        )

    def incoming(gr, i):
        source = lax.rem(z + i, streams)
        return remote(
            mixed.at[gr, source],
            spot(gr, source),
            out_send.at[source, gr],
            out_recv.at[source, gr],
            (t, source),
        )

    def own_out(gr):
        return pltpu.make_async_copy(mixed.at[gr, z], spot(gr, z), out_own.at[gr])

    far = list(reversed(near))

    def finish(gr):
        for i in far + [0]:
            dest = lax.rem(z + i, streams)
            for n in range(each):
                h = gr * each + n
                read = read_ref[dest, h] + dot3(query_ref[dest, h], prev[h], 1, 1)
                readout = read.astype(BF16).astype(F32)
                scale = lax.rsqrt(jnp.mean(readout * readout, -1, keepdims=True) + 1e-06)
                mixed[gr, dest, :, n * DV : (n + 1) * DV] = (
                    readout * scale * gain_ref[...]
                ).astype(BF16)
            if i == 0:
                own_out(gr).start()
            else:
                outgoing(gr, i).start()

    for gr in range(groups):
        join(gr)
    prefixes()
    for gr in range(groups):
        enter(gr)
        finish(gr)

    for gr in range(groups):
        own_out(gr).wait()
        for i in far:
            incoming(gr, i).wait_recv()
    for gr in range(groups):
        for i in far:
            outgoing(gr, i).wait_send()
        pair_copy(gr).wait_send()
        for source in range(chips - 1):

            @pl.when(chip == source)
            def _():
                for dest in range(chips - 1, source, -1):
                    to_chip(gr, source, dest).wait_send()

    def sent():
        drain(stage.at[pl.ds(0, streams - 1)], cross_send.at[0])
        for i in range(1, chips):
            drain(full.at[pl.ds(0, streams - 1), pl.ds(0, share)], plane_send.at[i])

    only(is_sender, sent)
    if paired:
        drain(full.at[pl.ds(0, streams - 1), pl.ds(0, origins * share)], pass_send.at[0])
    else:

        @pl.when(core == 0)
        def _():
            drain(full.at[pl.ds(0, streams - 1), pl.ds(0, origins * share)], pass_send.at[0])

    drain(gates.at[0, pl.ds(0, streams - 1)], gate_send.at[0])
    drain(gates.at[0, pl.ds(0, streams - 1)], gate_pass.at[0])
    for k in range(streams):

        @pl.when((z >= k) & (z < streams - 1))
        def _():
            drain(x_ref.at[z - k], right_sem.at[z - k])

        @pl.when((z + k < streams) & (z > 0))
        def _():
            drain(x_ref.at[z + k], left_sem.at[z + k])


def shards(
    tokens, w_query, w_key, w_value, decay_proj, beta_proj, decay_rate, beta_bias, norm_gain
):
    streams = lax.axis_size("stream")
    places = lax.axis_size("tm")
    heads = HEADS // streams
    depth = w_query.shape[0]
    senders = min(places, depth // 16)
    share = depth // senders
    local, features = tokens.shape
    chips = places // 2
    width = 3 * heads * DK
    groups = GROUPS if heads % GROUPS == 0 else 1
    any_space = pl.BlockSpec(memory_space=pl.ANY)
    vmem = pl.BlockSpec(memory_space=pltpu.VMEM)
    dma = pltpu.SemaphoreType.DMA
    return pl.pallas_call(
        functools.partial(layer_kernel, streams, places, heads, senders),
        out_shape=jax.ShapeDtypeStruct((local, HEADS * DV), BF16),
        in_specs=[any_space] * 6 + [vmem] * 3,
        out_specs=any_space,
        scratch_shapes=[
            pltpu.VMEM((streams, local, features), BF16),
            pltpu.VMEM((streams, depth, width), BF16),
            pltpu.VMEM((streams, share, width), BF16),
            pltpu.VMEM((2, streams, HEADS, depth), BF16),
            pltpu.VMEM((HEADS, CHUNK), F32),
            pltpu.VMEM((streams, heads, DK + DV, DK), F32),
            pltpu.VMEM((heads, DK + DV, DK), F32),
            pltpu.VMEM((streams, heads, CHUNK, DV), F32),
            pltpu.VMEM((streams, heads, CHUNK, DK), F32),
            pltpu.VMEM((heads, DK + DV, DK), BF16),
            pltpu.VMEM((heads, DK + DV, DK), BF16),
            pltpu.VMEM((heads, DK + DV, DK), BF16),
            pltpu.VMEM((chips, heads, DK + DV, DK), BF16),
            pltpu.VMEM((heads, DV, DK), F32),
            pltpu.VMEM((groups, streams, local, heads // groups * DV), BF16),
            dma((streams,)),
            dma((1,)),
            dma((1,)),
            dma((1,)),
            dma((1,)),
            dma((streams,)),
            dma((1,)),
            dma((1,)),
            dma((streams,)),
            dma((streams,)),
            dma((streams, PIECES)),
            dma((1,)),
            dma((streams,)),
            dma((chips,)),
            dma((senders, streams)),
            dma((1,)),
            dma((1,)),
            dma((groups,)),
            dma((groups,)),
            dma((chips, groups)),
            dma((chips, groups)),
            dma((streams, groups)),
            dma((streams, groups)),
            dma((groups,)),
        ],
        compiler_params=pltpu.CompilerParams(collective_id=0, has_side_effects=True),
    )(
        tokens,
        w_query,
        w_key,
        w_value,
        decay_proj.T,
        beta_proj.T,
        decay_rate[None],
        beta_bias[None],
        norm_gain[None],
    )


def solution(mesh):
    return jax.shard_map(
        shards,
        mesh=mesh,
        in_specs=(
            P(("tm", "stream"), None),
            P("stream", None),
            P("stream", None),
            P("stream", None),
            P("stream", None),
            P("stream", None),
            P(),
            P(),
            P(),
        ),
        out_specs=P(("tm", "stream"), None),
        check_vma=False,
    )
```

```python
import functools

import jax
import jax.numpy as jnp
from jax import lax
from jax.experimental import pallas as pl
from jax.experimental.pallas import tpu as pltpu
from jax.sharding import PartitionSpec as P

HEADS = 16
DK = 128
DV = 128
CHUNK = 128
PIECES = 4
F32 = jnp.float32
BF16 = jnp.bfloat16


def halves(a):
    high = a.astype(BF16)
    return high, (a - high.astype(F32)).astype(BF16)


def contract(a, b, dims):
    return lax.dot_general(a, b, dims, preferred_element_type=F32)


def dot3(a, b, ca, cb, batch=0):
    ah, al = halves(a)
    bh, bl = halves(b)
    free = batch + (cb - batch + 1) % 2
    lead = tuple(range(batch))
    wide = jnp.concatenate([bh, bl], free)
    both = contract(
        jnp.concatenate([ah, al], ca),
        jnp.concatenate([wide, wide], cb),
        (((ca,), (cb,)), (lead, lead)),
    )
    half = both.shape[-1] // 2
    return both[..., :half] + both[..., half:]


def dot2(a, b, ca, cb):
    ah, al = halves(a)
    return contract(
        jnp.concatenate([ah, al], ca), jnp.concatenate([b, b], cb), (((ca,), (cb,)), ((), ()))
    )


def around(count):
    return sorted(range(1, count), key=lambda i: min(i, count - i))


def layer_kernel(
    streams,
    places,
    heads,
    senders,
    tok_ref,
    wq_ref,
    wk_ref,
    wv_ref,
    dec_ref,
    bet_ref,
    rate_ref,
    bias_ref,
    gain_ref,
    out_ref,
    x_ref,
    full,
    stage,
    gates,
    cum_row,
    step_ref,
    run_ref,
    read_ref,
    query_ref,
    sent_map,
    sib_map,
    total,
    got,
    prev,
    state,
    mixed,
    load_sem,
    own_sem,
    gate_load,
    tok_load,
    gate_send,
    gate_recv,
    gate_pass,
    gate_sib,
    right_sem,
    left_sem,
    tok_recv,
    cross_send,
    cross_recv,
    plane_send,
    plane_recv,
    pass_send,
    sib_recv,
    pair_send,
    pair_recv,
    chip_send,
    chip_recv,
    back_send,
    back_recv,
    out_send,
    out_recv,
    out_own,
):
    t = lax.axis_index("tm")
    z = lax.axis_index("stream")
    chips = places // 2
    chip = t // 2
    core = t % 2
    sibling = chip * 2 + 1 - core
    depth = wq_ref.shape[0]
    share = depth // senders
    stride = places // senders
    step = max(stride // 2, 1)
    paired = stride == 1
    origins = senders // 2 if paired else senders
    base = chip // step * step
    local, features = tok_ref.shape
    part = local // PIECES
    near = around(streams)
    span = heads * DK
    halved = heads % 2 == 0
    each = heads // 2 if halved else heads

    def remote(src, dst, send, recv, device):
        return pltpu.make_async_remote_copy(
            src_ref=src,
            dst_ref=dst,
            send_sem=send,
            recv_sem=recv,
            device_id=device,
            device_id_type=pl.DeviceIdType.MESH,
        )

    def drain(ref, sem):
        pltpu.make_async_copy(ref, ref, sem).wait()

    def only(cond, body):
        if cond is True:
            body()
        elif cond is not False:
            pl.when(cond)(body)

    is_sender = True if paired else (t % stride == 0)
    active = True if paired else (core == 0)
    mine = t // stride

    def slot(i):
        at = lax.rem(base + i * step, chips)
        return 2 * at + core if paired else at // step

    weights = (wq_ref, wk_ref, wv_ref)
    my_rows = pl.ds(pl.multiple_of(mine * share, share), share)

    def load_stage():
        for i in near:
            dest = lax.rem(z + i, streams)
            for j, ref in enumerate(weights):
                pltpu.make_async_copy(
                    ref.at[my_rows, pl.ds(pl.multiple_of(dest * span, span), span)],
                    stage.at[dest, :, pl.ds(j * span, span)],
                    load_sem.at[dest],
                ).start()

    only(is_sender, load_stage)
    pltpu.make_async_copy(dec_ref, gates.at[0, z], gate_load.at[0]).start()
    pltpu.make_async_copy(bet_ref, gates.at[1, z], gate_load.at[0]).start()
    own_tok = pltpu.make_async_copy(tok_ref, x_ref.at[z], tok_load.at[0])
    own_tok.start()
    for j, ref in enumerate(weights):
        pltpu.make_async_copy(
            ref.at[:, pl.ds(pl.multiple_of(z * span, span), span)],
            full.at[z, :, pl.ds(j * span, span)],
            own_sem.at[0],
        ).start()

    others = [lax.rem(chip + i, chips) * 2 + core for i in range(1, chips)]
    peers = [(t, lax.rem(z + i, streams)) for i in near]
    peers += [(sibling, z)] + [(o, z) for o in others]
    barrier = pltpu.get_barrier_semaphore()
    for peer in peers:
        pl.semaphore_signal(
            barrier, inc=1, device_id=peer, device_id_type=pl.DeviceIdType.MESH
        )
    pl.semaphore_wait(barrier, len(peers))

    def rows_of(k):
        return pl.ds(pl.multiple_of(k * share, share), share)

    def line(s, p, right, first):
        at = pl.ds(p * part, part)
        src = tok_ref.at[at] if first else x_ref.at[s, at]
        send = (right_sem if right else left_sem).at[s]
        return remote(
            src, x_ref.at[s, at], send, tok_recv.at[s, p], (t, z + 1 if right else z - 1)
        )

    def gate_out(i):
        dest = lax.rem(z + i, streams)
        here = gates.at[core, z]
        return remote(here, here, gate_send.at[0], gate_recv.at[z], (t, dest))

    def gate_in(i):
        s = lax.rem(z + i, streams)
        here = gates.at[core, s]
        return remote(here, here, gate_send.at[0], gate_recv.at[s], (t, s))

    def gate_on(i):
        s = lax.rem(z + i, streams)
        here = gates.at[core, s]
        return remote(here, here, gate_pass.at[0], gate_sib.at[0], (sibling, z))

    def cross(i):
        dest = lax.rem(z + i, streams)
        return remote(
            stage.at[dest], full.at[z, rows_of(mine)], cross_send.at[0], cross_recv.at[z], (t, dest)
        )

    def crossed(i):
        s = lax.rem(z + i, streams)
        return remote(
            stage.at[s], full.at[s, rows_of(mine)], cross_send.at[0], cross_recv.at[s], (t, s)
        )

    def plane(i, s):
        here = full.at[s, rows_of(mine)]
        return remote(
            here, here, plane_send.at[i], plane_recv.at[mine, s], (others[i - 1], z)
        )

    def beside(k, s):
        here = full.at[s, rows_of(k)]
        return remote(here, here, pass_send.at[0], sib_recv.at[0], (sibling, z))

    def landed(k, s):
        here = full.at[s, rows_of(k)]
        return remote(here, here, plane_send.at[0], plane_recv.at[k, s], (others[0], z))

    def token_step(k, pieces):
        for p in pieces:

            @pl.when(z >= k)
            def _():
                line(z - k, p, True, False).wait_recv()

                @pl.when(z < streams - 1)
                def _():
                    line(z - k, p, True, False).start()

            @pl.when(z + k < streams)
            def _():
                line(z + k, p, False, False).wait_recv()

                @pl.when(z > 0)
                def _():
                    line(z + k, p, False, False).start()

    def send_shares():
        for i in near:
            drain(stage.at[lax.rem(z + i, streams)], load_sem.at[lax.rem(z + i, streams)])
            cross(i).start()

    only(is_sender, send_shares)
    drain(gates.at[:, z], gate_load.at[0])
    for i in near:
        gate_out(i).start()
    for p in range(PIECES):

        @pl.when(z < streams - 1)
        def _():
            line(z, p, True, True).start()

        @pl.when(z > 0)
        def _():
            line(z, p, False, True).start()

    def spread():
        for i in near:
            s = lax.rem(z + i, streams)
            crossed(i).wait_recv()
            for j in range(1, chips):
                plane(j, s).start()
            beside(mine, s).start()

    only(is_sender, spread)
    for i in near:
        gate_in(i).wait_recv()
        gate_on(i).start()

    def pass_on(i):
        if i == 0:
            if paired:
                return
            cond = active & (chip != base)
        else:
            cond = active
        k = slot(i)

        def body():
            for n in near:
                s = lax.rem(z + n, streams)
                landed(k, s).wait_recv()
                beside(k, s).start()

        only(cond, body)

    token_step(1, range(PIECES))
    for i in range(origins):
        pass_on(i)
    own_tok.wait()
    drain(full.at[z], own_sem.at[0])
    drain(gates.at[0, pl.ds(0, streams - 1)], gate_sib.at[0])
    only(
        True if paired else core == 1,
        lambda: drain(full.at[pl.ds(0, streams - 1), pl.ds(0, origins * share)], sib_recv.at[0]),
    )

    row_at = lax.broadcasted_iota(jnp.int32, (CHUNK, CHUNK), 0)
    col_at = lax.broadcasted_iota(jnp.int32, (CHUNK, CHUNK), 1)
    low = row_at >= col_at
    strict = row_at > col_at
    eye = jnp.where(row_at == col_at, 1.0, 0.0)
    lower_ones = jnp.where(low, 1.0, 0.0).astype(BF16)
    lane = lax.broadcasted_iota(jnp.int32, (CHUNK, HEADS), 1)

    def turn(n):
        fewer = jnp.minimum(z, streams - 1 - z)
        left = z * 2 >= streams
        both = n <= 2 * fewer
        k = jnp.where(both, (n + 1) // 2, n - fewer)
        leftward = jnp.where(both, jnp.where(left, n % 2 == 0, n % 2 == 1), left)
        at = jnp.where(leftward, z - k, z + k)
        return (z, None) if n == 0 else (at, leftward)

    def columns(a, first):
        picked = [
            jnp.sum(jnp.where(lane == z * heads + h, a, 0.0), -1, keepdims=True)
            for h in range(heads)
        ]
        return jnp.stack(picked)

    def split(a):
        return jnp.stack([a[:, h * DK : (h + 1) * DK] for h in range(heads)])

    def process(n):
        at, leftward = turn(n)
        x = x_ref[at]
        sums = None
        for s in range(streams):
            g2 = gates[:, s].reshape(2 * HEADS, depth)
            term = contract(x[:, s * depth : (s + 1) * depth], g2, (((1,), (1,)), ((), ())))
            sums = term if sums is None else sums + term
        first = sums[:, :HEADS]
        soft = jnp.maximum(first, 0.0) + jnp.log1p(jnp.exp(-jnp.abs(first)))
        decay = (-rate_ref[...] * soft).astype(BF16)
        beta = (1.0 / (1.0 + jnp.exp(-(sums[:, HEADS:] + bias_ref[...])))).astype(BF16).astype(F32)
        cum = contract(lower_ones, decay, (((1,), (0,)), ((), ())))
        cum_row[...] = cum.T
        g = columns(cum, 0)
        b = columns(beta, 0)
        g_row = jnp.stack([cum_row[pl.ds(z * heads + h, 1), :] for h in range(heads)])

        def project(j):
            w = full[:, :, j * span : (j + 1) * span].reshape(streams * depth, span)
            return split(contract(x, w, (((1,), (0,)), ((), ()))))

        raw_k = project(1)
        k = (raw_k * lax.rsqrt(jnp.sum(raw_k * raw_k, -1, keepdims=True) + 1e-06)).astype(BF16)
        raw_q = project(0)
        q = (
            raw_q * lax.rsqrt(jnp.sum(raw_q * raw_q, -1, keepdims=True) + 1e-06) * DK ** (-0.5)
        ).astype(BF16)
        v = project(2).astype(BF16).astype(F32)
        g_last = g[:, CHUNK - 1 :, :]
        growth = jnp.exp(g)
        tail = jnp.exp(g_last - g)
        whole = jnp.exp(g_last)

        pair = contract(jnp.concatenate([k, q], 1), k, (((2,), (2,)), ((0,), (0,))))
        spread_ = jnp.exp(jnp.where(low[None], g - g_row, 0.0))
        lmat = jnp.where(strict[None], b * spread_ * pair[:, :CHUNK], 0.0)
        mmat = jnp.where(low[None], spread_ * pair[:, CHUNK:], 0.0)

        inverse = None
        size = 1
        while size < CHUNK:
            inside = (row_at // (2 * size) == col_at // (2 * size)) & (
                row_at // size != col_at // size
            )
            off = jnp.where(inside[None], lmat, 0.0)
            if inverse is None:
                inverse = eye[None] - off
            else:
                inverse = inverse - dot3(inverse, dot3(off, inverse, 2, 1, 1), 2, 1, 1)
            size *= 2

        kf = k.astype(F32)
        right = jnp.concatenate([(b * growth) * kf, b * v], 2)
        wu = dot3(inverse, right, 2, 1, 1)
        jumps = dot3(jnp.swapaxes(wu, 1, 2), tail * kf, 2, 1, 1)
        step_map = jnp.concatenate([whole * eye[None] - jumps[:, :DK], jumps[:, DK:]], 1)
        step_ref[at] = step_map
        if n == 0:
            run = step_map
        else:
            run = run_ref[...]
            before = jnp.where(leftward, step_map, run)
            after = jnp.where(leftward, run, step_map)
            run = join_maps(before, after)
        if n < streams - 1:
            run_ref[...] = run
        else:
            sent_map[...] = run.astype(BF16)
            give(0).start()
            give_rest(lambda copy: copy.start())
            run_ref[...] = run
        mwu = dot3(mmat, wu, 2, 1, 1)
        query_ref[:, at] = growth * q.astype(F32) - mwu[:, :, :DK]
        read_ref[:, at] = mwu[:, :, DK:]

    def join_maps(before, after):
        both = dot3(before, after[:, :DK], 2, 1, 1)
        return jnp.concatenate([both[:, :DK], both[:, DK:] + after[:, DK:]], 1)

    mine_at = core * each if halved else 0
    theirs_at = (1 - core) * each if halved else 0

    def give(which):
        at = pl.ds(theirs_at if which == 0 else mine_at, each)
        return remote(
            sent_map.at[at], sib_map.at[at], pair_send.at[which], pair_recv.at[which], (sibling, z)
        )

    def taken(which):
        at = pl.ds(mine_at if which == 0 else theirs_at, each)
        return remote(
            sent_map.at[at], sib_map.at[at], pair_send.at[which], pair_recv.at[which], (sibling, z)
        )

    def give_rest(act):
        if halved:

            @pl.when(core == 0)
            def _():
                act(give(1))

    def to_chip(n, source, dest):
        src, dst = total.at[n], got.at[source, n]
        if source == 0:
            src, dst = total.at[n, pl.ds(DK, DV)], got.at[0, n, pl.ds(DK, DV)]
        return remote(
            src, dst, chip_send.at[dest, n], chip_recv.at[source, n], (dest * 2 + core, z)
        )

    def back(n, start):
        here = prev.at[start + n]
        return remote(here, here, back_send.at[n], back_recv.at[n], (sibling, z))

    for n in range(streams):
        process(n)
        if n == 0 and streams > 2:
            token_step(2, range(PIECES // 2))
        elif n == 1 and streams > 2:
            token_step(2, range(PIECES // 2, PIECES))
        elif 2 <= n < streams - 1:
            token_step(n + 1, range(PIECES))

    def carries():
        for c in range(1, streams - 1):
            step_ref[c] = join_maps(step_ref[c - 1], step_ref[c])

    def join():
        taken(0).wait_recv()

        @pl.when(chip < chips - 1)
        def _():
            at = pl.ds(mine_at, each)
            own = run_ref[at]
            other = sib_map[at].astype(F32)
            before = jnp.where(core == 0, own, other)
            after = jnp.where(core == 0, other, own)
            total[...] = join_maps(before, after).astype(BF16)

        for source in range(chips - 1):

            @pl.when(chip == source)
            def _():
                for n in range(each):
                    for dest in range(chips - 1, source, -1):
                        to_chip(n, source, dest).start()

    def prefixes():
        for c in range(1, streams):
            both = dot3(query_ref[:, c], step_ref[c - 1], 2, 2, 1)
            query_ref[:, c] = both[:, :, :DK]
            read_ref[:, c] = read_ref[:, c] + both[:, :, DK:]

    def enter(n):
        h = mine_at + n

        @pl.when(chip == 0)
        def _():
            prev[h] = jnp.zeros((DV, DK), F32)

        for source in range(chips - 1):

            @pl.when(chip > source)
            def _():
                to_chip(n, source, chip).wait_recv()
                if source == 0:
                    prev[h] = got[0, n, DK:].astype(F32)
                else:
                    prev[h] = dot2(prev[h], got[source, n, :DK], 1, 0) + got[
                        source, n, DK:
                    ].astype(F32)

        if halved:

            @pl.when(chip > 0)
            def _():
                back(n, mine_at).start()

    def hear(n):
        h = theirs_at + n

        @pl.when(chip == 0)
        def _():
            prev[h] = jnp.zeros((DV, DK), F32)

        @pl.when(chip > 0)
        def _():
            back(n, theirs_at).wait_recv()

    def spot(h, source):
        at = pl.multiple_of((source * heads + h) * DV, DV)
        return out_ref.at[:, pl.ds(at, DV)]

    def outgoing(h, i):
        dest = lax.rem(z + i, streams)
        return remote(
            mixed.at[h, dest], spot(h, z), out_send.at[0], out_recv.at[z], (t, dest)
        )

    def own_out(h):
        return pltpu.make_async_copy(mixed.at[h, z], spot(h, z), out_own.at[0])

    far = list(reversed(near))

    def finish(h):
        carried = prev[h]
        state[...] = carried

        @pl.when(core == 1)
        def _():
            state[...] = dot2(carried, sib_map[h, :DK], 1, 0) + sib_map[h, DK:].astype(F32)

        reads = dot3(query_ref[h].reshape(streams * local, DK), state[...], 1, 1)
        read = read_ref[h].reshape(streams * local, DV) + reads
        readout = read.astype(BF16).astype(F32)
        scale = lax.rsqrt(jnp.mean(readout * readout, -1, keepdims=True) + 1e-06)
        mixed[h] = (readout * scale * gain_ref[...]).astype(BF16).reshape(streams, local, DV)
        for i in far:
            outgoing(h, i).start()
        own_out(h).start()

    carries()
    join()
    prefixes()
    for n in range(each):
        enter(n)
        finish(mine_at + n)
    if halved:

        @pl.when(core == 1)
        def _():
            taken(1).wait_recv()

        for n in range(each):
            hear(n)
            finish(theirs_at + n)

    drain(mixed.at[:, 0], out_own.at[0])
    for i in far:
        drain(mixed.at[:, 0], out_recv.at[lax.rem(z + i, streams)])
    drain(mixed.at[:, pl.ds(0, streams - 1)], out_send.at[0])
    give(0).wait_send()
    give_rest(lambda copy: copy.wait_send())
    for n in range(each):
        for source in range(chips - 1):

            @pl.when(chip == source)
            def _():
                for dest in range(chips - 1, source, -1):
                    to_chip(n, source, dest).wait_send()

        if halved:

            @pl.when(chip > 0)
            def _():
                back(n, mine_at).wait_send()

    def sent():
        drain(stage.at[pl.ds(0, streams - 1)], cross_send.at[0])
        for i in range(1, chips):
            drain(full.at[pl.ds(0, streams - 1), pl.ds(0, share)], plane_send.at[i])

    only(is_sender, sent)
    if paired:
        drain(full.at[pl.ds(0, streams - 1), pl.ds(0, origins * share)], pass_send.at[0])
    else:

        @pl.when(core == 0)
        def _():
            drain(full.at[pl.ds(0, streams - 1), pl.ds(0, origins * share)], pass_send.at[0])

    drain(gates.at[0, pl.ds(0, streams - 1)], gate_send.at[0])
    drain(gates.at[0, pl.ds(0, streams - 1)], gate_pass.at[0])
    for k in range(streams):

        @pl.when((z >= k) & (z < streams - 1))
        def _():
            drain(x_ref.at[z - k], right_sem.at[z - k])

        @pl.when((z + k < streams) & (z > 0))
        def _():
            drain(x_ref.at[z + k], left_sem.at[z + k])


def shards(
    tokens, w_query, w_key, w_value, decay_proj, beta_proj, decay_rate, beta_bias, norm_gain
):
    streams = lax.axis_size("stream")
    places = lax.axis_size("tm")
    heads = HEADS // streams
    depth = w_query.shape[0]
    senders = min(places, depth // 16)
    share = depth // senders
    local, features = tokens.shape
    chips = places // 2
    width = 3 * heads * DK
    each = heads // 2 if heads % 2 == 0 else heads
    any_space = pl.BlockSpec(memory_space=pl.ANY)
    vmem = pl.BlockSpec(memory_space=pltpu.VMEM)
    dma = pltpu.SemaphoreType.DMA
    return pl.pallas_call(
        functools.partial(layer_kernel, streams, places, heads, senders),
        out_shape=jax.ShapeDtypeStruct((local, HEADS * DV), BF16),
        in_specs=[any_space] * 6 + [vmem] * 3,
        out_specs=any_space,
        scratch_shapes=[
            pltpu.VMEM((streams, local, features), BF16),
            pltpu.VMEM((streams, depth, width), BF16),
            pltpu.VMEM((streams, share, width), BF16),
            pltpu.VMEM((2, streams, HEADS, depth), BF16),
            pltpu.VMEM((HEADS, CHUNK), F32),
            pltpu.VMEM((streams, heads, DK + DV, DK), F32),
            pltpu.VMEM((heads, DK + DV, DK), F32),
            pltpu.VMEM((heads, streams, CHUNK, DV), F32),
            pltpu.VMEM((heads, streams, CHUNK, DK), F32),
            pltpu.VMEM((heads, DK + DV, DK), BF16),
            pltpu.VMEM((heads, DK + DV, DK), BF16),
            pltpu.VMEM((each, DK + DV, DK), BF16),
            pltpu.VMEM((chips, each, DK + DV, DK), BF16),
            pltpu.VMEM((heads, DV, DK), F32),
            pltpu.VMEM((DV, DK), F32),
            pltpu.VMEM((heads, streams, local, DV), BF16),
            dma((streams,)),
            dma((1,)),
            dma((1,)),
            dma((1,)),
            dma((1,)),
            dma((streams,)),
            dma((1,)),
            dma((1,)),
            dma((streams,)),
            dma((streams,)),
            dma((streams, PIECES)),
            dma((1,)),
            dma((streams,)),
            dma((chips,)),
            dma((senders, streams)),
            dma((1,)),
            dma((1,)),
            dma((2,)),
            dma((2,)),
            dma((chips, each)),
            dma((chips, each)),
            dma((each,)),
            dma((each,)),
            dma((1,)),
            dma((streams,)),
            dma((1,)),
        ],
        compiler_params=pltpu.CompilerParams(collective_id=0, has_side_effects=True),
    )(
        tokens,
        w_query,
        w_key,
        w_value,
        decay_proj.T,
        beta_proj.T,
        decay_rate[None],
        beta_bias[None],
        norm_gain[None],
    )


def solution(mesh):
    return jax.shard_map(
        shards,
        mesh=mesh,
        in_specs=(
            P(("tm", "stream"), None),
            P("stream", None),
            P("stream", None),
            P("stream", None),
            P("stream", None),
            P("stream", None),
            P(),
            P(),
            P(),
        ),
        out_specs=P(("tm", "stream"), None),
        check_vma=False,
    )
```

```python
import functools

import jax
import jax.numpy as jnp
from jax import lax
from jax.experimental import pallas as pl
from jax.experimental.pallas import tpu as pltpu
from jax.sharding import PartitionSpec as P

HEADS = 16
DK = 128
DV = 128
CHUNK = 128
PIECES = 4
DIRECT = 0
F32 = jnp.float32
BF16 = jnp.bfloat16


def halves(a):
    high = a.astype(BF16)
    return high, (a - high.astype(F32)).astype(BF16)


def contract(a, b, dims):
    return lax.dot_general(a, b, dims, preferred_element_type=F32)


def dot3(a, b, ca, cb, batch=0):
    ah, al = halves(a)
    bh, bl = halves(b)
    free = batch + (cb - batch + 1) % 2
    lead = tuple(range(batch))
    wide = jnp.concatenate([bh, bl], free)
    both = contract(
        jnp.concatenate([ah, al], ca),
        jnp.concatenate([wide, wide], cb),
        (((ca,), (cb,)), (lead, lead)),
    )
    half = both.shape[-1] // 2
    return both[..., :half] + both[..., half:]


def dot2(a, b, ca, cb):
    ah, al = halves(a)
    return contract(
        jnp.concatenate([ah, al], ca), jnp.concatenate([b, b], cb), (((ca,), (cb,)), ((), ()))
    )


def around(count):
    return sorted(range(1, count), key=lambda i: min(i, count - i))


def layer_kernel(
    streams,
    places,
    heads,
    senders,
    tok_ref,
    wq_ref,
    wk_ref,
    wv_ref,
    dec_ref,
    bet_ref,
    rate_ref,
    bias_ref,
    gain_ref,
    out_ref,
    x_ref,
    full,
    stage,
    gates,
    cum_row,
    k_ref,
    decays_ref,
    growth_ref,
    wu_ref,
    step_ref,
    run_ref,
    read_ref,
    query_ref,
    sent_map,
    sib_map,
    total,
    got,
    prev,
    state,
    mixed,
    load_sem,
    own_sem,
    gate_load,
    tok_load,
    gate_send,
    gate_recv,
    gate_pass,
    gate_sib,
    right_sem,
    left_sem,
    across_send,
    tok_recv,
    cross_send,
    cross_recv,
    plane_send,
    plane_recv,
    pass_send,
    sib_recv,
    pair_send,
    pair_recv,
    chip_send,
    chip_recv,
    back_send,
    back_recv,
    out_send,
    out_recv,
    out_own,
):
    t = lax.axis_index("tm")
    z = lax.axis_index("stream")
    chips = places // 2
    chip = t // 2
    core = t % 2
    sibling = chip * 2 + 1 - core
    depth = wq_ref.shape[0]
    share = depth // senders
    stride = places // senders
    step = max(stride // 2, 1)
    paired = stride == 1
    origins = senders // 2 if paired else senders
    base = chip // step * step
    local, features = tok_ref.shape
    part = local // PIECES
    near = around(streams)
    span = heads * DK
    halved = heads % 2 == 0
    each = heads // 2 if halved else heads

    def remote(src, dst, send, recv, device):
        return pltpu.make_async_remote_copy(
            src_ref=src,
            dst_ref=dst,
            send_sem=send,
            recv_sem=recv,
            device_id=device,
            device_id_type=pl.DeviceIdType.MESH,
        )

    def drain(ref, sem):
        pltpu.make_async_copy(ref, ref, sem).wait()

    def only(cond, body):
        if cond is True:
            body()
        elif cond is not False:
            pl.when(cond)(body)

    is_sender = True if paired else (t % stride == 0)
    active = True if paired else (core == 0)
    mine = t // stride

    def slot(i):
        at = lax.rem(base + i * step, chips)
        return 2 * at + core if paired else at // step

    weights = (wq_ref, wk_ref, wv_ref)
    my_rows = pl.ds(pl.multiple_of(mine * share, share), share)

    def load_stage():
        for i in near:
            dest = lax.rem(z + i, streams)
            for j, ref in enumerate(weights):
                pltpu.make_async_copy(
                    ref.at[my_rows, pl.ds(pl.multiple_of(dest * span, span), span)],
                    stage.at[dest, :, pl.ds(j * span, span)],
                    load_sem.at[dest],
                ).start()

    only(is_sender, load_stage)
    pltpu.make_async_copy(dec_ref, gates.at[0, z], gate_load.at[0]).start()
    pltpu.make_async_copy(bet_ref, gates.at[1, z], gate_load.at[0]).start()
    own_tok = pltpu.make_async_copy(tok_ref, x_ref.at[z], tok_load.at[0])
    own_tok.start()
    for j, ref in enumerate(weights):
        pltpu.make_async_copy(
            ref.at[:, pl.ds(pl.multiple_of(z * span, span), span)],
            full.at[z, :, pl.ds(j * span, span)],
            own_sem.at[0],
        ).start()

    square = chips == 4 and paired and share % 32 == 0
    if square:
        beyond = [chip + 1 - 2 * (chip % 2), lax.rem(chip + 2, chips), 3 - chip]
    else:
        beyond = [lax.rem(chip + i, chips) for i in range(1, chips)]
    others = [c * 2 + core for c in beyond]
    peers = [(t, lax.rem(z + i, streams)) for i in near]
    peers += [(sibling, z)] + [(o, z) for o in others]
    barrier = pltpu.get_barrier_semaphore()
    for peer in peers:
        pl.semaphore_signal(
            barrier, inc=1, device_id=peer, device_id_type=pl.DeviceIdType.MESH
        )
    pl.semaphore_wait(barrier, len(peers))

    def rows_of(k):
        return pl.ds(pl.multiple_of(k * share, share), share)

    def line(s, p, right, first):
        at = pl.ds(p * part, part)
        src = tok_ref.at[at] if first else x_ref.at[s, at]
        send = (right_sem if right else left_sem).at[s]
        return remote(
            src, x_ref.at[s, at], send, tok_recv.at[s, p], (t, z + 1 if right else z - 1)
        )

    def gate_out(i):
        dest = lax.rem(z + i, streams)
        here = gates.at[core, z]
        return remote(here, here, gate_send.at[0], gate_recv.at[z], (t, dest))

    def gate_in(i):
        s = lax.rem(z + i, streams)
        here = gates.at[core, s]
        return remote(here, here, gate_send.at[0], gate_recv.at[s], (t, s))

    def gate_on(i):
        s = lax.rem(z + i, streams)
        here = gates.at[core, s]
        return remote(here, here, gate_pass.at[0], gate_sib.at[0], (sibling, z))

    def cross(i):
        dest = lax.rem(z + i, streams)
        return remote(
            stage.at[dest], full.at[z, rows_of(mine)], cross_send.at[0], cross_recv.at[z], (t, dest)
        )

    def crossed(i):
        s = lax.rem(z + i, streams)
        return remote(
            stage.at[s], full.at[s, rows_of(mine)], cross_send.at[0], cross_recv.at[s], (t, s)
        )

    def plane(i, s):
        here = full.at[s, rows_of(mine)]
        return remote(
            here, here, plane_send.at[i], plane_recv.at[mine, s], (others[i - 1], z)
        )

    def beside(k, s):
        here = full.at[s, rows_of(k)]
        return remote(here, here, pass_send.at[0], sib_recv.at[0], (sibling, z))

    def landed(k, s):
        here = full.at[s, rows_of(k)]
        return remote(here, here, plane_send.at[0], plane_recv.at[k, s], (others[0], z))

    direct = range(PIECES - DIRECT, PIECES) if streams > 2 else range(0)

    def relayed(k, p):
        return not (k == streams - 2 and p in direct)

    def across(p):
        at = pl.ds(p * part, part)
        dest = jnp.where(z == 0, streams - 1, 0)
        return remote(
            tok_ref.at[at], x_ref.at[z, at], across_send.at[0], tok_recv.at[z, p], (t, dest)
        )

    def token_step(k, pieces):
        for p in pieces:

            @pl.when(z >= k)
            def _():
                line(z - k, p, True, False).wait_recv()

                if relayed(k, p):

                    @pl.when(z < streams - 1)
                    def _():
                        line(z - k, p, True, False).start()

            @pl.when(z + k < streams)
            def _():
                line(z + k, p, False, False).wait_recv()

                if relayed(k, p):

                    @pl.when(z > 0)
                    def _():
                        line(z + k, p, False, False).start()

    def send_shares():
        for i in near:
            drain(stage.at[lax.rem(z + i, streams)], load_sem.at[lax.rem(z + i, streams)])
            cross(i).start()

    only(is_sender, send_shares)
    drain(gates.at[:, z], gate_load.at[0])
    for i in near:
        gate_out(i).start()
    for p in range(PIECES):

        @pl.when(z < streams - 1)
        def _():
            line(z, p, True, True).start()

        @pl.when(z > 0)
        def _():
            line(z, p, False, True).start()

    @pl.when((z == 0) | (z == streams - 1))
    def _():
        for p in direct:
            across(p).start()

    def forward(i, s):
        at = pl.multiple_of((beyond[i - 1] * 2 + core) * share + (i - 1) * (share // 2), 16)
        here = full.at[s, pl.ds(at, share // 2)]
        k = beyond[i - 1] * 2 + core
        return remote(
            here, here, plane_send.at[3], plane_recv.at[k, s], (others[2 - i], z)
        )

    def spread(n):
        s = lax.rem(z + n, streams)
        crossed(n).wait_recv()
        for j in range(1, 3 if square else chips):
            plane(j, s).start()
        beside(mine, s).start()

    def pass_on(i, n):
        if i == 0:
            if paired:
                return
            cond = active & (chip != base)
        else:
            cond = active
        k = beyond[i - 1] * 2 + core if square else slot(i)

        def body():
            s = lax.rem(z + n, streams)
            landed(k, s).wait_recv()
            if square and i < 3:
                forward(i, s).start()
            beside(k, s).start()

        only(cond, body)

    def share_gates():
        for i in near:
            gate_in(i).wait_recv()
            gate_on(i).start()

    if square:
        for at, n in enumerate(near):
            spread(n)
            if at > 0:
                pass_on(1, near[at - 1])
                pass_on(2, near[at - 1])
        share_gates()
        for n in near[:-2]:
            pass_on(3, n)
        token_step(1, [0])
        pass_on(1, near[-1])
        pass_on(2, near[-1])
        for p, n in enumerate(near[-2:]):
            pass_on(3, n)
            token_step(1, [p + 1])
        token_step(1, range(1 + len(near[-2:]), PIECES))
    else:
        for n in near:
            only(is_sender, functools.partial(spread, n))
        share_gates()
        token_step(1, range(PIECES))
        for n in near:
            for i in range(origins):
                pass_on(i, n)
    own_tok.wait()
    drain(full.at[z], own_sem.at[0])
    drain(gates.at[0, pl.ds(0, streams - 1)], gate_sib.at[0])
    only(
        True if paired else core == 1,
        lambda: drain(full.at[pl.ds(0, streams - 1), pl.ds(0, origins * share)], sib_recv.at[0]),
    )

    row_at = lax.broadcasted_iota(jnp.int32, (CHUNK, CHUNK), 0)
    col_at = lax.broadcasted_iota(jnp.int32, (CHUNK, CHUNK), 1)
    low = row_at >= col_at
    strict = row_at > col_at
    eye = jnp.where(row_at == col_at, 1.0, 0.0)
    lower_ones = jnp.where(low, 1.0, 0.0).astype(BF16)
    lane = lax.broadcasted_iota(jnp.int32, (CHUNK, HEADS), 1)

    def turn(n):
        fewer = jnp.minimum(z, streams - 1 - z)
        left = z * 2 >= streams
        both = n <= 2 * fewer
        k = jnp.where(both, (n + 1) // 2, n - fewer)
        leftward = jnp.where(both, jnp.where(left, n % 2 == 0, n % 2 == 1), left)
        at = jnp.where(leftward, z - k, z + k)
        return (z, None) if n == 0 else (at, leftward)

    def columns(a, first):
        picked = [
            jnp.sum(jnp.where(lane == z * heads + h, a, 0.0), -1, keepdims=True)
            for h in range(heads)
        ]
        return jnp.stack(picked)

    def split(a):
        return jnp.stack([a[:, h * DK : (h + 1) * DK] for h in range(heads)])

    def project(x, j):
        w = full[:, :, j * span : (j + 1) * span].reshape(streams * depth, span)
        return split(contract(x, w, (((1,), (0,)), ((), ()))))

    def reads(n):
        at, _ = turn(n)
        raw_q = project(x_ref[at], 0)
        q = (
            raw_q * lax.rsqrt(jnp.sum(raw_q * raw_q, -1, keepdims=True) + 1e-06) * DK ** (-0.5)
        ).astype(BF16)
        scores = contract(q, k_ref[...], (((2,), (2,)), ((0,), (0,))))
        mwu = dot3(decays_ref[...] * scores, wu_ref[...], 2, 1, 1)
        query_ref[:, at] = growth_ref[...] * q.astype(F32) - mwu[:, :, :DK]
        read_ref[:, at] = mwu[:, :, DK:]

    def process(n):
        at, leftward = turn(n)
        x = x_ref[at]
        sums = None
        for s in range(streams):
            g2 = gates[:, s].reshape(2 * HEADS, depth)
            term = contract(x[:, s * depth : (s + 1) * depth], g2, (((1,), (1,)), ((), ())))
            sums = term if sums is None else sums + term
        first = sums[:, :HEADS]
        soft = jnp.maximum(first, 0.0) + jnp.log1p(jnp.exp(-jnp.abs(first)))
        decay = (-rate_ref[...] * soft).astype(BF16)
        beta = (1.0 / (1.0 + jnp.exp(-(sums[:, HEADS:] + bias_ref[...])))).astype(BF16).astype(F32)
        cum = contract(lower_ones, decay, (((1,), (0,)), ((), ())))
        cum_row[...] = cum.T
        g = columns(cum, 0)
        b = columns(beta, 0)
        g_row = jnp.stack([cum_row[pl.ds(z * heads + h, 1), :] for h in range(heads)])

        raw_k = project(x, 1)
        k = (raw_k * lax.rsqrt(jnp.sum(raw_k * raw_k, -1, keepdims=True) + 1e-06)).astype(BF16)
        v = project(x, 2).astype(BF16).astype(F32)
        g_last = g[:, CHUNK - 1 :, :]
        growth = jnp.exp(g)
        tail = jnp.exp(g_last - g)
        whole = jnp.exp(g_last)

        pair = contract(k, k, (((2,), (2,)), ((0,), (0,))))
        decays = jnp.exp(jnp.where(low[None], g - g_row, 0.0))
        lmat = jnp.where(strict[None], b * decays * pair, 0.0)
        k_ref[...] = k
        decays_ref[...] = jnp.where(low[None], decays, 0.0)
        growth_ref[...] = jnp.broadcast_to(growth, (heads, CHUNK, DK))

        inverse = None
        size = 1
        while size < CHUNK:
            inside = (row_at // (2 * size) == col_at // (2 * size)) & (
                row_at // size != col_at // size
            )
            off = jnp.where(inside[None], lmat, 0.0)
            if inverse is None:
                inverse = eye[None] - off
            else:
                inverse = inverse - dot3(inverse, dot3(off, inverse, 2, 1, 1), 2, 1, 1)
            size *= 2

        kf = k.astype(F32)
        right = jnp.concatenate([(b * growth) * kf, b * v], 2)
        wu = dot3(inverse, right, 2, 1, 1)
        wu_ref[...] = wu
        jumps = dot3(jnp.swapaxes(wu, 1, 2), tail * kf, 2, 1, 1)
        step_map = jnp.concatenate([whole * eye[None] - jumps[:, :DK], jumps[:, DK:]], 1)
        step_ref[at] = step_map
        if n == 0:
            run = step_map
        else:
            run = run_ref[...]
            before = jnp.where(leftward, step_map, run)
            after = jnp.where(leftward, run, step_map)
            run = join_maps(before, after)
        if n < streams - 1:
            run_ref[...] = run
        else:
            sent_map[...] = run.astype(BF16)
            give(0).start()
            give_rest(lambda copy: copy.start())
            run_ref[...] = run

    def join_maps(before, after):
        both = dot3(before, after[:, :DK], 2, 1, 1)
        return jnp.concatenate([both[:, :DK], both[:, DK:] + after[:, DK:]], 1)

    mine_at = core * each if halved else 0
    theirs_at = (1 - core) * each if halved else 0

    def give(which):
        at = pl.ds(theirs_at if which == 0 else mine_at, each)
        return remote(
            sent_map.at[at], sib_map.at[at], pair_send.at[which], pair_recv.at[which], (sibling, z)
        )

    def taken(which):
        at = pl.ds(mine_at if which == 0 else theirs_at, each)
        return remote(
            sent_map.at[at], sib_map.at[at], pair_send.at[which], pair_recv.at[which], (sibling, z)
        )

    def give_rest(act):
        if halved:

            @pl.when(core == 0)
            def _():
                act(give(1))

    def to_chip(n, source, dest):
        src, dst = total.at[n], got.at[source, n]
        if source == 0:
            src, dst = total.at[n, pl.ds(DK, DV)], got.at[0, n, pl.ds(DK, DV)]
        return remote(
            src, dst, chip_send.at[dest, n], chip_recv.at[source, n], (dest * 2 + core, z)
        )

    def back(n, start):
        here = prev.at[start + n]
        return remote(here, here, back_send.at[n], back_recv.at[n], (sibling, z))

    for n in range(streams):
        process(n)
        if n == 0 and streams > 2:
            token_step(2, [0])
        if n < streams - 1:
            reads(n)
        if n == 0 and streams > 2:
            token_step(2, range(1, PIECES // 2))
        elif n == 1 and streams > 2:
            token_step(2, range(PIECES // 2, PIECES))
        elif 2 <= n < streams - 1:
            token_step(n + 1, range(PIECES))

    def carries():
        for c in range(1, streams - 1):
            step_ref[c] = join_maps(step_ref[c - 1], step_ref[c])

    def join():
        taken(0).wait_recv()

        @pl.when(chip < chips - 1)
        def _():
            at = pl.ds(mine_at, each)
            own = run_ref[at]
            other = sib_map[at].astype(F32)
            before = jnp.where(core == 0, own, other)
            after = jnp.where(core == 0, other, own)
            total[...] = join_maps(before, after).astype(BF16)

        for source in range(chips - 1):

            @pl.when(chip == source)
            def _():
                for n in range(each):
                    for dest in range(chips - 1, source, -1):
                        to_chip(n, source, dest).start()

    def prefixes():
        for c in range(1, streams):
            both = dot3(query_ref[:, c], step_ref[c - 1], 2, 2, 1)
            query_ref[:, c] = both[:, :, :DK]
            read_ref[:, c] = read_ref[:, c] + both[:, :, DK:]

    def enter(n):
        h = mine_at + n

        @pl.when(chip == 0)
        def _():
            prev[h] = jnp.zeros((DV, DK), F32)

        for source in range(chips - 1):

            @pl.when(chip > source)
            def _():
                to_chip(n, source, chip).wait_recv()
                if source == 0:
                    prev[h] = got[0, n, DK:].astype(F32)
                else:
                    prev[h] = dot2(prev[h], got[source, n, :DK], 1, 0) + got[
                        source, n, DK:
                    ].astype(F32)

        if halved:

            @pl.when(chip > 0)
            def _():
                back(n, mine_at).start()

    def hear(n):
        h = theirs_at + n

        @pl.when(chip == 0)
        def _():
            prev[h] = jnp.zeros((DV, DK), F32)

        @pl.when(chip > 0)
        def _():
            back(n, theirs_at).wait_recv()

    def spot(h, source):
        at = pl.multiple_of((source * heads + h) * DV, DV)
        return out_ref.at[:, pl.ds(at, DV)]

    def outgoing(h, i):
        dest = lax.rem(z + i, streams)
        return remote(
            mixed.at[h, dest], spot(h, z), out_send.at[0], out_recv.at[z], (t, dest)
        )

    def own_out(h):
        return pltpu.make_async_copy(mixed.at[h, z], spot(h, z), out_own.at[0])

    far = list(reversed(near))

    def finish(h):
        carried = prev[h]
        state[...] = carried

        @pl.when(core == 1)
        def _():
            state[...] = dot2(carried, sib_map[h, :DK], 1, 0) + sib_map[h, DK:].astype(F32)

        reads = dot3(query_ref[h].reshape(streams * local, DK), state[...], 1, 1)
        read = read_ref[h].reshape(streams * local, DV) + reads
        readout = read.astype(BF16).astype(F32)
        scale = lax.rsqrt(jnp.mean(readout * readout, -1, keepdims=True) + 1e-06)
        mixed[h] = (readout * scale * gain_ref[...]).astype(BF16).reshape(streams, local, DV)
        for i in far:
            outgoing(h, i).start()
        own_out(h).start()

    join()
    reads(streams - 1)
    carries()
    prefixes()
    for n in range(each):
        enter(n)
        finish(mine_at + n)
    if halved:

        @pl.when(core == 1)
        def _():
            taken(1).wait_recv()

        for n in range(each):
            hear(n)
            finish(theirs_at + n)

    drain(mixed.at[:, 0], out_own.at[0])
    for i in far:
        drain(mixed.at[:, 0], out_recv.at[lax.rem(z + i, streams)])
    drain(mixed.at[:, pl.ds(0, streams - 1)], out_send.at[0])
    give(0).wait_send()
    give_rest(lambda copy: copy.wait_send())
    for n in range(each):
        for source in range(chips - 1):

            @pl.when(chip == source)
            def _():
                for dest in range(chips - 1, source, -1):
                    to_chip(n, source, dest).wait_send()

        if halved:

            @pl.when(chip > 0)
            def _():
                back(n, mine_at).wait_send()

    def sent():
        drain(stage.at[pl.ds(0, streams - 1)], cross_send.at[0])
        for i in range(1, chips):
            drain(full.at[pl.ds(0, streams - 1), pl.ds(0, share)], plane_send.at[i])

    only(is_sender, sent)
    if paired:
        drain(full.at[pl.ds(0, streams - 1), pl.ds(0, origins * share)], pass_send.at[0])
    else:

        @pl.when(core == 0)
        def _():
            drain(full.at[pl.ds(0, streams - 1), pl.ds(0, origins * share)], pass_send.at[0])

    drain(gates.at[0, pl.ds(0, streams - 1)], gate_send.at[0])
    drain(gates.at[0, pl.ds(0, streams - 1)], gate_pass.at[0])

    def whole_of(k):
        return local - part * len(direct) if k == streams - 2 else local

    if len(direct) > 0:

        @pl.when((z == 0) | (z == streams - 1))
        def _():
            drain(x_ref.at[z, pl.ds(0, part * len(direct))], across_send.at[0])

    for k in range(streams):

        @pl.when((z >= k) & (z < streams - 1))
        def _():
            drain(x_ref.at[z - k, pl.ds(0, whole_of(k))], right_sem.at[z - k])

        @pl.when((z + k < streams) & (z > 0))
        def _():
            drain(x_ref.at[z + k, pl.ds(0, whole_of(k))], left_sem.at[z + k])


def shards(
    tokens, w_query, w_key, w_value, decay_proj, beta_proj, decay_rate, beta_bias, norm_gain
):
    streams = lax.axis_size("stream")
    places = lax.axis_size("tm")
    heads = HEADS // streams
    depth = w_query.shape[0]
    senders = min(places, depth // 16)
    share = depth // senders
    local, features = tokens.shape
    chips = places // 2
    width = 3 * heads * DK
    each = heads // 2 if heads % 2 == 0 else heads
    any_space = pl.BlockSpec(memory_space=pl.ANY)
    vmem = pl.BlockSpec(memory_space=pltpu.VMEM)
    dma = pltpu.SemaphoreType.DMA
    return pl.pallas_call(
        functools.partial(layer_kernel, streams, places, heads, senders),
        out_shape=jax.ShapeDtypeStruct((local, HEADS * DV), BF16),
        in_specs=[any_space] * 6 + [vmem] * 3,
        out_specs=any_space,
        scratch_shapes=[
            pltpu.VMEM((streams, local, features), BF16),
            pltpu.VMEM((streams, depth, width), BF16),
            pltpu.VMEM((streams, share, width), BF16),
            pltpu.VMEM((2, streams, HEADS, depth), BF16),
            pltpu.VMEM((HEADS, CHUNK), F32),
            pltpu.VMEM((heads, CHUNK, DK), BF16),
            pltpu.VMEM((heads, CHUNK, CHUNK), F32),
            pltpu.VMEM((heads, CHUNK, DK), F32),
            pltpu.VMEM((heads, CHUNK, DK + DV), F32),
            pltpu.VMEM((streams, heads, DK + DV, DK), F32),
            pltpu.VMEM((heads, DK + DV, DK), F32),
            pltpu.VMEM((heads, streams, CHUNK, DV), F32),
            pltpu.VMEM((heads, streams, CHUNK, DK), F32),
            pltpu.VMEM((heads, DK + DV, DK), BF16),
            pltpu.VMEM((heads, DK + DV, DK), BF16),
            pltpu.VMEM((each, DK + DV, DK), BF16),
            pltpu.VMEM((chips, each, DK + DV, DK), BF16),
            pltpu.VMEM((heads, DV, DK), F32),
            pltpu.VMEM((DV, DK), F32),
            pltpu.VMEM((heads, streams, local, DV), BF16),
            dma((streams,)),
            dma((1,)),
            dma((1,)),
            dma((1,)),
            dma((1,)),
            dma((streams,)),
            dma((1,)),
            dma((1,)),
            dma((streams,)),
            dma((streams,)),
            dma((1,)),
            dma((streams, PIECES)),
            dma((1,)),
            dma((streams,)),
            dma((chips,)),
            dma((senders, streams)),
            dma((1,)),
            dma((1,)),
            dma((2,)),
            dma((2,)),
            dma((chips, each)),
            dma((chips, each)),
            dma((each,)),
            dma((each,)),
            dma((1,)),
            dma((streams,)),
            dma((1,)),
        ],
        compiler_params=pltpu.CompilerParams(collective_id=0, has_side_effects=True),
    )(
        tokens,
        w_query,
        w_key,
        w_value,
        decay_proj.T,
        beta_proj.T,
        decay_rate[None],
        beta_bias[None],
        norm_gain[None],
    )


def solution(mesh):
    return jax.shard_map(
        shards,
        mesh=mesh,
        in_specs=(
            P(("tm", "stream"), None),
            P("stream", None),
            P("stream", None),
            P("stream", None),
            P("stream", None),
            P("stream", None),
            P(),
            P(),
            P(),
        ),
        out_specs=P(("tm", "stream"), None),
        check_vma=False,
    )
```

```python
import functools

import jax
import jax.numpy as jnp
from jax import lax
from jax.experimental import pallas as pl
from jax.experimental.pallas import tpu as pltpu
from jax.sharding import PartitionSpec as P

HEADS = 16
DK = 128
DV = 128
CHUNK = 128
PIECES = 4
DIRECT = 0
F32 = jnp.float32
BF16 = jnp.bfloat16


def halves(a):
    high = a.astype(BF16)
    return high, (a - high.astype(F32)).astype(BF16)


def contract(a, b, dims):
    return lax.dot_general(a, b, dims, preferred_element_type=F32)


def dot3(a, b, ca, cb, batch=0):
    ah, al = halves(a)
    bh, bl = halves(b)
    free = batch + (cb - batch + 1) % 2
    lead = tuple(range(batch))
    wide = jnp.concatenate([bh, bl], free)
    both = contract(
        jnp.concatenate([ah, al], ca),
        jnp.concatenate([wide, wide], cb),
        (((ca,), (cb,)), (lead, lead)),
    )
    half = both.shape[-1] // 2
    return both[..., :half] + both[..., half:]


def dot2(a, b):
    bh, bl = halves(b)
    return contract(
        jnp.concatenate([a, a], 1), jnp.concatenate([bh, bl], 0), (((1,), (0,)), ((), ()))
    )


def around(count):
    return sorted(range(1, count), key=lambda i: min(i, count - i))


def layer_kernel(
    streams,
    places,
    heads,
    senders,
    tok_ref,
    wq_ref,
    wk_ref,
    wv_ref,
    dec_ref,
    bet_ref,
    rate_ref,
    bias_ref,
    gain_ref,
    out_ref,
    x_ref,
    full,
    stage,
    gates,
    cum_row,
    k_ref,
    decays_ref,
    growth_ref,
    wu_ref,
    step_ref,
    run_ref,
    read_ref,
    query_ref,
    sent_map,
    sib_map,
    total,
    got,
    prev,
    state,
    mixed,
    load_sem,
    own_sem,
    gate_load,
    tok_load,
    gate_send,
    gate_recv,
    gate_pass,
    gate_sib,
    right_sem,
    left_sem,
    across_send,
    tok_recv,
    cross_send,
    cross_recv,
    plane_send,
    plane_recv,
    pass_send,
    sib_recv,
    pair_send,
    pair_recv,
    chip_send,
    chip_recv,
    back_send,
    back_recv,
    out_send,
    out_recv,
    out_own,
):
    t = lax.axis_index("tm")
    z = lax.axis_index("stream")
    chips = places // 2
    chip = t // 2
    core = t % 2
    sibling = chip * 2 + 1 - core
    depth = wq_ref.shape[0]
    share = depth // senders
    stride = places // senders
    step = max(stride // 2, 1)
    paired = stride == 1
    origins = senders // 2 if paired else senders
    base = chip // step * step
    local, features = tok_ref.shape
    part = local // PIECES
    near = around(streams)
    span = heads * DK
    halved = heads % 2 == 0
    each = heads // 2 if halved else heads

    def remote(src, dst, send, recv, device):
        return pltpu.make_async_remote_copy(
            src_ref=src,
            dst_ref=dst,
            send_sem=send,
            recv_sem=recv,
            device_id=device,
            device_id_type=pl.DeviceIdType.MESH,
        )

    def drain(ref, sem):
        pltpu.make_async_copy(ref, ref, sem).wait()

    def only(cond, body):
        if cond is True:
            body()
        elif cond is not False:
            pl.when(cond)(body)

    is_sender = True if paired else (t % stride == 0)
    active = True if paired else (core == 0)
    mine = t // stride

    def slot(i):
        at = lax.rem(base + i * step, chips)
        return 2 * at + core if paired else at // step

    weights = (wq_ref, wk_ref, wv_ref)
    my_rows = pl.ds(pl.multiple_of(mine * share, share), share)

    def load_stage():
        for i in near:
            dest = lax.rem(z + i, streams)
            for j, ref in enumerate(weights):
                pltpu.make_async_copy(
                    ref.at[my_rows, pl.ds(pl.multiple_of(dest * span, span), span)],
                    stage.at[dest, :, pl.ds(j * span, span)],
                    load_sem.at[dest],
                ).start()

    only(is_sender, load_stage)
    pltpu.make_async_copy(dec_ref, gates.at[0, z], gate_load.at[0]).start()
    pltpu.make_async_copy(bet_ref, gates.at[1, z], gate_load.at[0]).start()
    own_tok = pltpu.make_async_copy(tok_ref, x_ref.at[z], tok_load.at[0])
    own_tok.start()
    for j, ref in enumerate(weights):
        pltpu.make_async_copy(
            ref.at[:, pl.ds(pl.multiple_of(z * span, span), span)],
            full.at[z, :, pl.ds(j * span, span)],
            own_sem.at[0],
        ).start()

    square = chips == 4 and paired and share % 32 == 0
    if square:
        beyond = [chip + 1 - 2 * (chip % 2), lax.rem(chip + 2, chips), 3 - chip]
    else:
        beyond = [lax.rem(chip + i, chips) for i in range(1, chips)]
    others = [c * 2 + core for c in beyond]
    peers = [(t, lax.rem(z + i, streams)) for i in near]
    peers += [(sibling, z)] + [(o, z) for o in others]
    barrier = pltpu.get_barrier_semaphore()
    for peer in peers:
        pl.semaphore_signal(
            barrier, inc=1, device_id=peer, device_id_type=pl.DeviceIdType.MESH
        )
    pl.semaphore_wait(barrier, len(peers))

    def rows_of(k):
        return pl.ds(pl.multiple_of(k * share, share), share)

    def line(s, p, right, first):
        at = pl.ds(p * part, part)
        src = tok_ref.at[at] if first else x_ref.at[s, at]
        send = (right_sem if right else left_sem).at[s]
        return remote(
            src, x_ref.at[s, at], send, tok_recv.at[s, p], (t, z + 1 if right else z - 1)
        )

    def gate_out(i):
        dest = lax.rem(z + i, streams)
        here = gates.at[core, z]
        return remote(here, here, gate_send.at[0], gate_recv.at[z], (t, dest))

    def gate_in(i):
        s = lax.rem(z + i, streams)
        here = gates.at[core, s]
        return remote(here, here, gate_send.at[0], gate_recv.at[s], (t, s))

    def gate_on(i):
        s = lax.rem(z + i, streams)
        here = gates.at[core, s]
        return remote(here, here, gate_pass.at[0], gate_sib.at[0], (sibling, z))

    def cross(i):
        dest = lax.rem(z + i, streams)
        return remote(
            stage.at[dest], full.at[z, rows_of(mine)], cross_send.at[0], cross_recv.at[z], (t, dest)
        )

    def crossed(i):
        s = lax.rem(z + i, streams)
        return remote(
            stage.at[s], full.at[s, rows_of(mine)], cross_send.at[0], cross_recv.at[s], (t, s)
        )

    def plane(i, s):
        here = full.at[s, rows_of(mine)]
        return remote(
            here, here, plane_send.at[i], plane_recv.at[mine, s], (others[i - 1], z)
        )

    def beside(k, s):
        here = full.at[s, rows_of(k)]
        return remote(here, here, pass_send.at[0], sib_recv.at[0], (sibling, z))

    def landed(k, s):
        here = full.at[s, rows_of(k)]
        return remote(here, here, plane_send.at[0], plane_recv.at[k, s], (others[0], z))

    direct = range(PIECES - DIRECT, PIECES) if streams > 2 else range(0)

    def relayed(k, p):
        return not (k == streams - 2 and p in direct)

    def across(p):
        at = pl.ds(p * part, part)
        dest = jnp.where(z == 0, streams - 1, 0)
        return remote(
            tok_ref.at[at], x_ref.at[z, at], across_send.at[0], tok_recv.at[z, p], (t, dest)
        )

    def token_step(k, pieces):
        for p in pieces:

            @pl.when(z >= k)
            def _():
                line(z - k, p, True, False).wait_recv()

                if relayed(k, p):

                    @pl.when(z < streams - 1)
                    def _():
                        line(z - k, p, True, False).start()

            @pl.when(z + k < streams)
            def _():
                line(z + k, p, False, False).wait_recv()

                if relayed(k, p):

                    @pl.when(z > 0)
                    def _():
                        line(z + k, p, False, False).start()

    def send_shares():
        for i in near:
            drain(stage.at[lax.rem(z + i, streams)], load_sem.at[lax.rem(z + i, streams)])
            cross(i).start()

    only(is_sender, send_shares)
    drain(gates.at[:, z], gate_load.at[0])
    for i in near:
        gate_out(i).start()
    for p in range(PIECES):

        @pl.when(z < streams - 1)
        def _():
            line(z, p, True, True).start()

        @pl.when(z > 0)
        def _():
            line(z, p, False, True).start()

    @pl.when((z == 0) | (z == streams - 1))
    def _():
        for p in direct:
            across(p).start()

    def quarter(i):
        return range(i * (PIECES // 4), (i + 1) * (PIECES // 4))

    def forward(i, s):
        at = pl.multiple_of((beyond[i - 1] * 2 + core) * share + (i - 1) * (share // 2), 16)
        here = full.at[s, pl.ds(at, share // 2)]
        k = beyond[i - 1] * 2 + core
        return remote(
            here, here, plane_send.at[3], plane_recv.at[k, s], (others[2 - i], z)
        )

    def spread(n):
        s = lax.rem(z + n, streams)
        crossed(n).wait_recv()
        for j in range(1, 3 if square else chips):
            plane(j, s).start()
        beside(mine, s).start()

    def pass_on(i, n):
        if i == 0:
            if paired:
                return
            cond = active & (chip != base)
        else:
            cond = active
        k = beyond[i - 1] * 2 + core if square else slot(i)

        def body():
            s = lax.rem(z + n, streams)
            landed(k, s).wait_recv()
            if square and i < 3:
                forward(i, s).start()
            beside(k, s).start()

        only(cond, body)

    def share_gates():
        for i in near:
            gate_in(i).wait_recv()
            gate_on(i).start()

    if square:
        for at, n in enumerate(near):
            spread(n)
            if at > 0:
                pass_on(1, near[at - 1])
                pass_on(2, near[at - 1])
        share_gates()
        for n in near[:-2]:
            pass_on(3, n)
        token_step(1, quarter(0))
        pass_on(1, near[-1])
        pass_on(2, near[-1])
        for p, n in enumerate(near[-2:]):
            pass_on(3, n)
            token_step(1, quarter(p + 1))
        token_step(1, range((1 + len(near[-2:])) * (PIECES // 4), PIECES))
    else:
        for n in near:
            only(is_sender, functools.partial(spread, n))
        share_gates()
        token_step(1, range(PIECES))
        for n in near:
            for i in range(origins):
                pass_on(i, n)
    own_tok.wait()
    drain(full.at[z], own_sem.at[0])
    drain(gates.at[0, pl.ds(0, streams - 1)], gate_sib.at[0])
    only(
        True if paired else core == 1,
        lambda: drain(full.at[pl.ds(0, streams - 1), pl.ds(0, origins * share)], sib_recv.at[0]),
    )

    row_at = lax.broadcasted_iota(jnp.int32, (CHUNK, CHUNK), 0)
    col_at = lax.broadcasted_iota(jnp.int32, (CHUNK, CHUNK), 1)
    low = row_at >= col_at
    strict = row_at > col_at
    eye = jnp.where(row_at == col_at, 1.0, 0.0)
    lower_ones = jnp.where(low, 1.0, 0.0).astype(BF16)
    lane = lax.broadcasted_iota(jnp.int32, (CHUNK, HEADS), 1)

    def turn(n):
        fewer = jnp.minimum(z, streams - 1 - z)
        left = z * 2 >= streams
        both = n <= 2 * fewer
        k = jnp.where(both, (n + 1) // 2, n - fewer)
        leftward = jnp.where(both, jnp.where(left, n % 2 == 0, n % 2 == 1), left)
        at = jnp.where(leftward, z - k, z + k)
        return (z, None) if n == 0 else (at, leftward)

    def columns(a, first):
        picked = [
            jnp.sum(jnp.where(lane == z * heads + h, a, 0.0), -1, keepdims=True)
            for h in range(heads)
        ]
        return jnp.stack(picked)

    def split(a):
        return jnp.stack([a[:, h * DK : (h + 1) * DK] for h in range(heads)])

    def project(x, j):
        w = full[:, :, j * span : (j + 1) * span].reshape(streams * depth, span)
        return split(contract(x, w, (((1,), (0,)), ((), ()))))

    def reads(n):
        at, _ = turn(n)
        raw_q = project(x_ref[at], 0)
        q = (
            raw_q * lax.rsqrt(jnp.sum(raw_q * raw_q, -1, keepdims=True) + 1e-06) * DK ** (-0.5)
        ).astype(BF16)
        scores = contract(q, k_ref[...], (((2,), (2,)), ((0,), (0,))))
        mwu = dot3(decays_ref[...] * scores, wu_ref[...], 2, 1, 1)
        query_ref[:, at] = growth_ref[...] * q.astype(F32) - mwu[:, :, :DK]
        read_ref[:, at] = mwu[:, :, DK:]

    def process(n):
        at, leftward = turn(n)
        x = x_ref[at]
        sums = None
        for s in range(streams):
            g2 = gates[:, s].reshape(2 * HEADS, depth)
            term = contract(x[:, s * depth : (s + 1) * depth], g2, (((1,), (1,)), ((), ())))
            sums = term if sums is None else sums + term
        first = sums[:, :HEADS]
        soft = jnp.maximum(first, 0.0) + jnp.log1p(jnp.exp(-jnp.abs(first)))
        decay = (-rate_ref[...] * soft).astype(BF16)
        beta = (1.0 / (1.0 + jnp.exp(-(sums[:, HEADS:] + bias_ref[...])))).astype(BF16).astype(F32)
        cum = contract(lower_ones, decay, (((1,), (0,)), ((), ())))
        cum_row[...] = cum.T
        g = columns(cum, 0)
        b = columns(beta, 0)
        g_row = jnp.stack([cum_row[pl.ds(z * heads + h, 1), :] for h in range(heads)])

        raw_k = project(x, 1)
        k = (raw_k * lax.rsqrt(jnp.sum(raw_k * raw_k, -1, keepdims=True) + 1e-06)).astype(BF16)
        v = project(x, 2).astype(BF16).astype(F32)
        g_last = g[:, CHUNK - 1 :, :]
        growth = jnp.exp(g)
        tail = jnp.exp(g_last - g_row)
        whole = jnp.exp(g_last)

        pair = contract(k, k, (((2,), (2,)), ((0,), (0,))))
        decays = jnp.exp(jnp.where(low[None], g - g_row, 0.0))
        lmat = jnp.where(strict[None], b * decays * pair, 0.0)
        k_ref[...] = k
        decays_ref[...] = jnp.where(low[None], decays, 0.0)
        growth_ref[...] = jnp.broadcast_to(growth, (heads, CHUNK, DK))

        inverse = None
        size = 1
        while size < CHUNK:
            inside = (row_at // (2 * size) == col_at // (2 * size)) & (
                row_at // size != col_at // size
            )
            off = jnp.where(inside[None], lmat, 0.0)
            if inverse is None:
                inverse = eye[None] - off
            else:
                inverse = inverse - dot3(inverse, dot3(off, inverse, 2, 1, 1), 2, 1, 1)
            size *= 2

        kf = k.astype(F32)
        right = jnp.concatenate([(b * growth) * kf, b * v], 2)
        wu = dot3(inverse, right, 2, 1, 1)
        wu_ref[...] = wu
        jumps = dot3(tail * jnp.swapaxes(kf, 1, 2), wu, 2, 1, 1)
        step_map = jnp.concatenate([whole * eye[None] - jumps[:, :, :DK], jumps[:, :, DK:]], 2)
        step_ref[at] = step_map
        if n == 0:
            run = step_map
        else:
            run = run_ref[...]
            before = jnp.where(leftward, step_map, run)
            after = jnp.where(leftward, run, step_map)
            run = join_maps(before, after)
        if n < streams - 1:
            run_ref[...] = run
        else:
            sent_map[...] = run.astype(BF16)
            give(0).start()
            give_rest(lambda copy: copy.start())
            run_ref[...] = run

    def join_maps(before, after):
        both = dot3(after[:, :, :DK], before, 2, 1, 1)
        return jnp.concatenate([both[:, :, :DK], both[:, :, DK:] + after[:, :, DK:]], 2)

    mine_at = core * each if halved else 0
    theirs_at = (1 - core) * each if halved else 0

    def give(which):
        at = pl.ds(theirs_at if which == 0 else mine_at, each)
        return remote(
            sent_map.at[at], sib_map.at[at], pair_send.at[which], pair_recv.at[which], (sibling, z)
        )

    def taken(which):
        at = pl.ds(mine_at if which == 0 else theirs_at, each)
        return remote(
            sent_map.at[at], sib_map.at[at], pair_send.at[which], pair_recv.at[which], (sibling, z)
        )

    def give_rest(act):
        if halved:

            @pl.when(core == 0)
            def _():
                act(give(1))

    def to_chip(n, source, dest):
        src, dst = total.at[n], got.at[source, n]
        if source == 0:
            src, dst = total.at[n, :, pl.ds(DK, DV)], got.at[0, n, :, pl.ds(DK, DV)]
        return remote(
            src, dst, chip_send.at[dest, n], chip_recv.at[source, n], (dest * 2 + core, z)
        )

    def back(n, start):
        here = prev.at[start + n]
        return remote(here, here, back_send.at[n], back_recv.at[n], (sibling, z))

    for n in range(streams):
        process(n)
        if n < 2 < streams:
            token_step(2, quarter(2 * n))
        if n < streams - 1:
            reads(n)
        if n < 2 < streams:
            token_step(2, quarter(2 * n + 1))
        elif 2 <= n < streams - 1:
            token_step(n + 1, range(PIECES))

    def carries():
        for c in range(1, streams - 1):
            step_ref[c] = join_maps(step_ref[c - 1], step_ref[c])

    def join():
        taken(0).wait_recv()

        @pl.when(chip < chips - 1)
        def _():
            at = pl.ds(mine_at, each)
            own = run_ref[at]
            other = sib_map[at].astype(F32)
            before = jnp.where(core == 0, own, other)
            after = jnp.where(core == 0, other, own)
            total[...] = join_maps(before, after).astype(BF16)

        for source in range(chips - 1):

            @pl.when(chip == source)
            def _():
                for n in range(each):
                    for dest in range(chips - 1, source, -1):
                        to_chip(n, source, dest).start()

    def prefixes():
        for c in range(1, streams):
            both = dot3(query_ref[:, c], step_ref[c - 1], 2, 1, 1)
            query_ref[:, c] = both[:, :, :DK]
            read_ref[:, c] = read_ref[:, c] + both[:, :, DK:]

    def enter(n):
        h = mine_at + n

        @pl.when(chip == 0)
        def _():
            prev[h] = jnp.zeros((DK, DV), F32)

        for source in range(chips - 1):

            @pl.when(chip > source)
            def _():
                to_chip(n, source, chip).wait_recv()
                if source == 0:
                    prev[h] = got[0, n, :, DK:].astype(F32)
                else:
                    prev[h] = dot2(got[source, n, :, :DK], prev[h]) + got[
                        source, n, :, DK:
                    ].astype(F32)

        if halved:

            @pl.when(chip > 0)
            def _():
                back(n, mine_at).start()

    def hear(n):
        h = theirs_at + n

        @pl.when(chip == 0)
        def _():
            prev[h] = jnp.zeros((DK, DV), F32)

        @pl.when(chip > 0)
        def _():
            back(n, theirs_at).wait_recv()

    def spot(h, source):
        at = pl.multiple_of((source * heads + h) * DV, DV)
        return out_ref.at[:, pl.ds(at, DV)]

    def outgoing(h, i):
        dest = lax.rem(z + i, streams)
        return remote(
            mixed.at[h, dest], spot(h, z), out_send.at[0], out_recv.at[z], (t, dest)
        )

    def own_out(h):
        return pltpu.make_async_copy(mixed.at[h, z], spot(h, z), out_own.at[0])

    far = list(reversed(near))

    def finish(h):
        carried = prev[h]
        state[...] = carried

        @pl.when(core == 1)
        def _():
            state[...] = dot2(sib_map[h, :, :DK], carried) + sib_map[h, :, DK:].astype(F32)

        reads = dot3(query_ref[h].reshape(streams * local, DK), state[...], 1, 0)
        read = read_ref[h].reshape(streams * local, DV) + reads
        readout = read.astype(BF16).astype(F32)
        scale = lax.rsqrt(jnp.mean(readout * readout, -1, keepdims=True) + 1e-06)
        mixed[h] = (readout * scale * gain_ref[...]).astype(BF16).reshape(streams, local, DV)
        for i in far:
            outgoing(h, i).start()
        own_out(h).start()

    join()
    reads(streams - 1)
    carries()
    prefixes()
    for n in range(each):
        enter(n)
        finish(mine_at + n)
    if halved:

        @pl.when(core == 1)
        def _():
            taken(1).wait_recv()

        for n in range(each):
            hear(n)
            finish(theirs_at + n)

    drain(mixed.at[:, 0], out_own.at[0])
    for i in far:
        drain(mixed.at[:, 0], out_recv.at[lax.rem(z + i, streams)])
    drain(mixed.at[:, pl.ds(0, streams - 1)], out_send.at[0])
    give(0).wait_send()
    give_rest(lambda copy: copy.wait_send())
    for n in range(each):
        for source in range(chips - 1):

            @pl.when(chip == source)
            def _():
                for dest in range(chips - 1, source, -1):
                    to_chip(n, source, dest).wait_send()

        if halved:

            @pl.when(chip > 0)
            def _():
                back(n, mine_at).wait_send()

    def sent():
        drain(stage.at[pl.ds(0, streams - 1)], cross_send.at[0])
        for i in range(1, chips):
            drain(full.at[pl.ds(0, streams - 1), pl.ds(0, share)], plane_send.at[i])

    only(is_sender, sent)
    if paired:
        drain(full.at[pl.ds(0, streams - 1), pl.ds(0, origins * share)], pass_send.at[0])
    else:

        @pl.when(core == 0)
        def _():
            drain(full.at[pl.ds(0, streams - 1), pl.ds(0, origins * share)], pass_send.at[0])

    drain(gates.at[0, pl.ds(0, streams - 1)], gate_send.at[0])
    drain(gates.at[0, pl.ds(0, streams - 1)], gate_pass.at[0])

    def whole_of(k):
        return local - part * len(direct) if k == streams - 2 else local

    if len(direct) > 0:

        @pl.when((z == 0) | (z == streams - 1))
        def _():
            drain(x_ref.at[z, pl.ds(0, part * len(direct))], across_send.at[0])

    for k in range(streams):

        @pl.when((z >= k) & (z < streams - 1))
        def _():
            drain(x_ref.at[z - k, pl.ds(0, whole_of(k))], right_sem.at[z - k])

        @pl.when((z + k < streams) & (z > 0))
        def _():
            drain(x_ref.at[z + k, pl.ds(0, whole_of(k))], left_sem.at[z + k])


def shards(
    tokens, w_query, w_key, w_value, decay_proj, beta_proj, decay_rate, beta_bias, norm_gain
):
    streams = lax.axis_size("stream")
    places = lax.axis_size("tm")
    heads = HEADS // streams
    depth = w_query.shape[0]
    senders = min(places, depth // 16)
    share = depth // senders
    local, features = tokens.shape
    chips = places // 2
    width = 3 * heads * DK
    each = heads // 2 if heads % 2 == 0 else heads
    any_space = pl.BlockSpec(memory_space=pl.ANY)
    vmem = pl.BlockSpec(memory_space=pltpu.VMEM)
    dma = pltpu.SemaphoreType.DMA
    return pl.pallas_call(
        functools.partial(layer_kernel, streams, places, heads, senders),
        out_shape=pltpu.VMEM((local, HEADS * DV), BF16),
        in_specs=[any_space] * 6 + [vmem] * 3,
        out_specs=vmem,
        scratch_shapes=[
            pltpu.VMEM((streams, local, features), BF16),
            pltpu.VMEM((streams, depth, width), BF16),
            pltpu.VMEM((streams, share, width), BF16),
            pltpu.VMEM((2, streams, HEADS, depth), BF16),
            pltpu.VMEM((HEADS, CHUNK), F32),
            pltpu.VMEM((heads, CHUNK, DK), BF16),
            pltpu.VMEM((heads, CHUNK, CHUNK), F32),
            pltpu.VMEM((heads, CHUNK, DK), F32),
            pltpu.VMEM((heads, CHUNK, DK + DV), F32),
            pltpu.VMEM((streams, heads, DK, DK + DV), F32),
            pltpu.VMEM((heads, DK, DK + DV), F32),
            pltpu.VMEM((heads, streams, CHUNK, DV), F32),
            pltpu.VMEM((heads, streams, CHUNK, DK), F32),
            pltpu.VMEM((heads, DK, DK + DV), BF16),
            pltpu.VMEM((heads, DK, DK + DV), BF16),
            pltpu.VMEM((each, DK, DK + DV), BF16),
            pltpu.VMEM((chips, each, DK, DK + DV), BF16),
            pltpu.VMEM((heads, DK, DV), F32),
            pltpu.VMEM((DK, DV), F32),
            pltpu.VMEM((heads, streams, local, DV), BF16),
            dma((streams,)),
            dma((1,)),
            dma((1,)),
            dma((1,)),
            dma((1,)),
            dma((streams,)),
            dma((1,)),
            dma((1,)),
            dma((streams,)),
            dma((streams,)),
            dma((1,)),
            dma((streams, PIECES)),
            dma((1,)),
            dma((streams,)),
            dma((chips,)),
            dma((senders, streams)),
            dma((1,)),
            dma((1,)),
            dma((2,)),
            dma((2,)),
            dma((chips, each)),
            dma((chips, each)),
            dma((each,)),
            dma((each,)),
            dma((1,)),
            dma((streams,)),
            dma((1,)),
        ],
        compiler_params=pltpu.CompilerParams(collective_id=0, has_side_effects=True),
    )(
        tokens,
        w_query,
        w_key,
        w_value,
        decay_proj.T,
        beta_proj.T,
        decay_rate[None],
        beta_bias[None],
        norm_gain[None],
    )


def solution(mesh):
    return jax.shard_map(
        shards,
        mesh=mesh,
        in_specs=(
            P(("tm", "stream"), None),
            P("stream", None),
            P("stream", None),
            P("stream", None),
            P("stream", None),
            P("stream", None),
            P(),
            P(),
            P(),
        ),
        out_specs=P(("tm", "stream"), None),
        check_vma=False,
    )
```

```python
import functools

import jax
import jax.numpy as jnp
from jax import lax
from jax.experimental import pallas as pl
from jax.experimental.pallas import tpu as pltpu
from jax.sharding import PartitionSpec as P

HEADS = 16
DK = 128
DV = 128
CHUNK = 128
PIECES = 4
DIRECT = 0
F32 = jnp.float32
BF16 = jnp.bfloat16


def halves(a):
    high = a.astype(BF16)
    return high, (a - high.astype(F32)).astype(BF16)


def contract(a, b, dims):
    return lax.dot_general(a, b, dims, preferred_element_type=F32)


def dot3(a, b, ca, cb, batch=0):
    ah, al = halves(a)
    bh, bl = halves(b)
    free = batch + (cb - batch + 1) % 2
    lead = tuple(range(batch))
    wide = jnp.concatenate([bh, bl], free)
    both = contract(
        jnp.concatenate([ah, al], ca),
        jnp.concatenate([wide, wide], cb),
        (((ca,), (cb,)), (lead, lead)),
    )
    half = both.shape[-1] // 2
    return both[..., :half] + both[..., half:]


def dot2(a, b):
    bh, bl = halves(b)
    return contract(
        jnp.concatenate([a, a], 1), jnp.concatenate([bh, bl], 0), (((1,), (0,)), ((), ()))
    )


def around(count):
    return sorted(range(1, count), key=lambda i: min(i, count - i))


def layer_kernel(
    streams,
    places,
    heads,
    senders,
    tok_ref,
    wq_ref,
    wk_ref,
    wv_ref,
    dec_ref,
    bet_ref,
    rate_ref,
    bias_ref,
    gain_ref,
    out_ref,
    x_ref,
    full,
    stage,
    gates,
    cum_row,
    k_ref,
    decays_ref,
    growth_ref,
    wu_ref,
    step_ref,
    run_ref,
    read_ref,
    query_ref,
    sent_map,
    sib_map,
    total,
    got,
    prev,
    state,
    mixed,
    load_sem,
    own_sem,
    gate_load,
    tok_load,
    gate_send,
    gate_recv,
    gate_pass,
    gate_sib,
    right_sem,
    left_sem,
    across_send,
    tok_recv,
    cross_send,
    cross_recv,
    plane_send,
    plane_recv,
    pass_send,
    sib_recv,
    pair_send,
    pair_recv,
    chip_send,
    chip_recv,
    back_send,
    back_recv,
    out_send,
    out_recv,
    out_own,
):
    t = lax.axis_index("tm")
    z = lax.axis_index("stream")
    chips = places // 2
    chip = t // 2
    core = t % 2
    sibling = chip * 2 + 1 - core
    depth = wq_ref.shape[0]
    share = depth // senders
    stride = places // senders
    step = max(stride // 2, 1)
    paired = stride == 1
    origins = senders // 2 if paired else senders
    base = chip // step * step
    local, features = tok_ref.shape
    part = local // PIECES
    near = around(streams)
    ranks = range(1, streams)
    span = heads * DK
    halved = heads % 2 == 0
    each = heads // 2 if halved else heads

    def remote(src, dst, send, recv, device):
        return pltpu.make_async_remote_copy(
            src_ref=src,
            dst_ref=dst,
            send_sem=send,
            recv_sem=recv,
            device_id=device,
            device_id_type=pl.DeviceIdType.MESH,
        )

    def drain(ref, sem):
        pltpu.make_async_copy(ref, ref, sem).wait()

    def only(cond, body):
        if cond is True:
            body()
        elif cond is not False:
            pl.when(cond)(body)

    is_sender = True if paired else (t % stride == 0)
    active = True if paired else (core == 0)
    mine = t // stride

    def slot(i):
        at = lax.rem(base + i * step, chips)
        return 2 * at + core if paired else at // step

    def turn(n):
        fewer = jnp.minimum(z, streams - 1 - z)
        left = z * 2 >= streams
        both = n <= 2 * fewer
        k = jnp.where(both, (n + 1) // 2, n - fewer)
        leftward = jnp.where(both, jnp.where(left, n % 2 == 0, n % 2 == 1), left)
        at = jnp.where(leftward, z - k, z + k)
        return (z, None) if n == 0 else (at, leftward)

    def partner(n):
        return turn(n)[0]

    weights = (wq_ref, wk_ref, wv_ref)
    my_rows = pl.ds(pl.multiple_of(mine * share, share), share)

    def load_stage():
        for i in near:
            dest = lax.rem(z + i, streams)
            for j, ref in enumerate(weights):
                pltpu.make_async_copy(
                    ref.at[my_rows, pl.ds(pl.multiple_of(dest * span, span), span)],
                    stage.at[dest, :, pl.ds(j * span, span)],
                    load_sem.at[dest],
                ).start()

    only(is_sender, load_stage)
    pltpu.make_async_copy(dec_ref, gates.at[0, z], gate_load.at[0]).start()
    pltpu.make_async_copy(bet_ref, gates.at[1, z], gate_load.at[0]).start()
    own_tok = pltpu.make_async_copy(tok_ref, x_ref.at[z], tok_load.at[0])
    own_tok.start()
    for j, ref in enumerate(weights):
        pltpu.make_async_copy(
            ref.at[:, pl.ds(pl.multiple_of(z * span, span), span)],
            full.at[z, :, pl.ds(j * span, span)],
            own_sem.at[0],
        ).start()

    square = chips == 4 and paired and share % 32 == 0
    if square:
        beyond = [chip + 1 - 2 * (chip % 2), lax.rem(chip + 2, chips), 3 - chip]
    else:
        beyond = [lax.rem(chip + i, chips) for i in range(1, chips)]
    others = [c * 2 + core for c in beyond]
    peers = [(t, lax.rem(z + i, streams)) for i in near]
    peers += [(sibling, z)] + [(o, z) for o in others]
    barrier = pltpu.get_barrier_semaphore()
    for peer in peers:
        pl.semaphore_signal(
            barrier, inc=1, device_id=peer, device_id_type=pl.DeviceIdType.MESH
        )
    pl.semaphore_wait(barrier, len(peers))

    def rows_of(k):
        return pl.ds(pl.multiple_of(k * share, share), share)

    def line(s, p, right, first):
        at = pl.ds(p * part, part)
        src = tok_ref.at[at] if first else x_ref.at[s, at]
        send = (right_sem if right else left_sem).at[s]
        return remote(
            src, x_ref.at[s, at], send, tok_recv.at[s, p], (t, z + 1 if right else z - 1)
        )

    def gate_out(i):
        dest = lax.rem(z + i, streams)
        here = gates.at[core, z]
        return remote(here, here, gate_send.at[0], gate_recv.at[z], (t, dest))

    def gate_in(i):
        s = lax.rem(z + i, streams)
        here = gates.at[core, s]
        return remote(here, here, gate_send.at[0], gate_recv.at[s], (t, s))

    def gate_on(i):
        s = lax.rem(z + i, streams)
        here = gates.at[core, s]
        return remote(here, here, gate_pass.at[0], gate_sib.at[0], (sibling, z))

    def cross(i):
        dest = lax.rem(z + i, streams)
        return remote(
            stage.at[dest], full.at[z, rows_of(mine)], cross_send.at[0], cross_recv.at[z], (t, dest)
        )

    def crossed(i):
        s = lax.rem(z + i, streams)
        return remote(
            stage.at[s], full.at[s, rows_of(mine)], cross_send.at[0], cross_recv.at[s], (t, s)
        )

    def origin(k):
        return k // 2 if paired else k

    def plane(i, s):
        here = full.at[s, rows_of(mine)]
        return remote(
            here, here, plane_send.at[i], plane_recv.at[origin(mine), s], (others[i - 1], z)
        )

    def beside(k, s):
        here = full.at[s, rows_of(k)]
        return remote(here, here, pass_send.at[0], sib_recv.at[0], (sibling, z))

    def landed(k, s):
        here = full.at[s, rows_of(k)]
        return remote(here, here, plane_send.at[0], plane_recv.at[origin(k), s], (others[0], z))

    direct = range(PIECES - DIRECT, PIECES) if streams > 2 else range(0)

    def relayed(k, p):
        return not (k == streams - 2 and p in direct)

    def across(p):
        at = pl.ds(p * part, part)
        dest = jnp.where(z == 0, streams - 1, 0)
        return remote(
            tok_ref.at[at], x_ref.at[z, at], across_send.at[0], tok_recv.at[z, p], (t, dest)
        )

    def token_step(k, pieces):
        for p in pieces:

            @pl.when(z >= k)
            def _():
                line(z - k, p, True, False).wait_recv()

                if relayed(k, p):

                    @pl.when(z < streams - 1)
                    def _():
                        line(z - k, p, True, False).start()

            @pl.when(z + k < streams)
            def _():
                line(z + k, p, False, False).wait_recv()

                if relayed(k, p):

                    @pl.when(z > 0)
                    def _():
                        line(z + k, p, False, False).start()

    def send_shares():
        for i in near:
            drain(stage.at[lax.rem(z + i, streams)], load_sem.at[lax.rem(z + i, streams)])
            cross(i).start()

    only(is_sender, send_shares)
    drain(gates.at[:, z], gate_load.at[0])
    for i in near:
        gate_out(i).start()
    for p in range(PIECES):

        @pl.when(z < streams - 1)
        def _():
            line(z, p, True, True).start()

        @pl.when(z > 0)
        def _():
            line(z, p, False, True).start()

    @pl.when((z == 0) | (z == streams - 1))
    def _():
        for p in direct:
            across(p).start()

    def quarter(i):
        return range(i * (PIECES // 4), (i + 1) * (PIECES // 4))

    def forward(i, s):
        at = pl.multiple_of((beyond[i - 1] * 2 + core) * share + (i - 1) * (share // 2), 16)
        here = full.at[s, pl.ds(at, share // 2)]
        k = beyond[i - 1] * 2 + core
        return remote(
            here, here, plane_send.at[3], plane_recv.at[origin(k), s], (others[2 - i], z)
        )

    def spread(n):
        s = lax.rem(z + n, streams)
        crossed(n).wait_recv()
        for j in range(1, 3 if square else chips):
            plane(j, s).start()
        beside(mine, s).start()

    def pass_on(i, n):
        if i == 0:
            if paired:
                return
            cond = active & (chip != base)
        else:
            cond = active
        k = beyond[i - 1] * 2 + core if square else slot(i)

        def body():
            s = lax.rem(z + n, streams)
            landed(k, s).wait_recv()
            if square and i < 3:
                forward(i, s).start()
            beside(k, s).start()

        only(cond, body)

    def share_gates():
        for i in near:
            gate_in(i).wait_recv()
            gate_on(i).start()

    if square:
        for at, n in enumerate(near):
            spread(n)
            if at > 0:
                pass_on(1, near[at - 1])
                pass_on(2, near[at - 1])
        share_gates()
        for n in near[:-2]:
            pass_on(3, n)
        token_step(1, quarter(0))
        pass_on(1, near[-1])
        pass_on(2, near[-1])
        for p, n in enumerate(near[-2:]):
            pass_on(3, n)
            token_step(1, quarter(p + 1))
        token_step(1, range((1 + len(near[-2:])) * (PIECES // 4), PIECES))
    else:
        for n in near:
            only(is_sender, functools.partial(spread, n))
        share_gates()
        token_step(1, range(PIECES))
        for n in near:
            for i in range(origins):
                pass_on(i, n)
    own_tok.wait()
    drain(full.at[z], own_sem.at[0])
    drain(gates.at[0, pl.ds(0, streams - 1)], gate_sib.at[0])
    only(
        True if paired else core == 1,
        lambda: drain(full.at[pl.ds(0, streams - 1), pl.ds(0, origins * share)], sib_recv.at[0]),
    )

    row_at = lax.broadcasted_iota(jnp.int32, (CHUNK, CHUNK), 0)
    col_at = lax.broadcasted_iota(jnp.int32, (CHUNK, CHUNK), 1)
    low = row_at >= col_at
    strict = row_at > col_at
    eye = jnp.where(row_at == col_at, 1.0, 0.0)
    lower_ones = jnp.where(low, 1.0, 0.0).astype(BF16)
    lane = lax.broadcasted_iota(jnp.int32, (CHUNK, HEADS), 1)

    def columns(a, first):
        picked = [
            jnp.sum(jnp.where(lane == z * heads + h, a, 0.0), -1, keepdims=True)
            for h in range(heads)
        ]
        return jnp.stack(picked)

    def split(a):
        return jnp.stack([a[:, h * DK : (h + 1) * DK] for h in range(heads)])

    def project(x, j):
        w = full[:, :, j * span : (j + 1) * span].reshape(streams * depth, span)
        return split(contract(x, w, (((1,), (0,)), ((), ()))))

    def reads(n):
        at, _ = turn(n)
        raw_q = project(x_ref[at], 0)
        q = (
            raw_q * lax.rsqrt(jnp.sum(raw_q * raw_q, -1, keepdims=True) + 1e-06) * DK ** (-0.5)
        ).astype(BF16)
        scores = contract(q, k_ref[...], (((2,), (2,)), ((0,), (0,))))
        mwu = dot3(decays_ref[...] * scores, wu_ref[...], 2, 1, 1)
        query_ref[:, at] = growth_ref[...] * q.astype(F32) - mwu[:, :, :DK]
        read_ref[:, at] = mwu[:, :, DK:]

    def process(n):
        at, leftward = turn(n)
        x = x_ref[at]
        sums = None
        for s in range(streams):
            g2 = gates[:, s].reshape(2 * HEADS, depth)
            term = contract(x[:, s * depth : (s + 1) * depth], g2, (((1,), (1,)), ((), ())))
            sums = term if sums is None else sums + term
        first = sums[:, :HEADS]
        soft = jnp.maximum(first, 0.0) + jnp.log1p(jnp.exp(-jnp.abs(first)))
        decay = (-rate_ref[...] * soft).astype(BF16)
        beta = (1.0 / (1.0 + jnp.exp(-(sums[:, HEADS:] + bias_ref[...])))).astype(BF16).astype(F32)
        cum = contract(lower_ones, decay, (((1,), (0,)), ((), ())))
        cum_row[...] = cum.T
        g = columns(cum, 0)
        b = columns(beta, 0)
        g_row = jnp.stack([cum_row[pl.ds(z * heads + h, 1), :] for h in range(heads)])

        raw_k = project(x, 1)
        k = (raw_k * lax.rsqrt(jnp.sum(raw_k * raw_k, -1, keepdims=True) + 1e-06)).astype(BF16)
        v = project(x, 2).astype(BF16).astype(F32)
        g_last = g[:, CHUNK - 1 :, :]
        growth = jnp.exp(g)
        tail = jnp.exp(g_last - g_row)
        whole = jnp.exp(g_last)

        pair = contract(k, k, (((2,), (2,)), ((0,), (0,))))
        decays = jnp.exp(jnp.where(low[None], g - g_row, 0.0))
        lmat = jnp.where(strict[None], b * decays * pair, 0.0)
        k_ref[...] = k
        decays_ref[...] = jnp.where(low[None], decays, 0.0)
        growth_ref[...] = jnp.broadcast_to(growth, (heads, CHUNK, DK))

        inverse = None
        size = 1
        while size < CHUNK:
            inside = (row_at // (2 * size) == col_at // (2 * size)) & (
                row_at // size != col_at // size
            )
            off = jnp.where(inside[None], lmat, 0.0)
            if inverse is None:
                inverse = eye[None] - off
            else:
                inverse = inverse - dot3(inverse, dot3(off, inverse, 2, 1, 1), 2, 1, 1)
            size *= 2

        kf = k.astype(F32)
        right = jnp.concatenate([(b * growth) * kf, b * v], 2)
        wu = dot3(inverse, right, 2, 1, 1)
        wu_ref[...] = wu
        jumps = dot3(tail * jnp.swapaxes(kf, 1, 2), wu, 2, 1, 1)
        step_map = jnp.concatenate([whole * eye[None] - jumps[:, :, :DK], jumps[:, :, DK:]], 2)
        step_ref[at] = step_map
        if n == 0:
            run = step_map
        else:
            run = run_ref[...]
            before = jnp.where(leftward, step_map, run)
            after = jnp.where(leftward, run, step_map)
            run = join_maps(before, after)
        if n < streams - 1:
            run_ref[...] = run
        else:
            sent_map[...] = run.astype(BF16)
            give(0).start()
            give_rest(lambda copy: copy.start())
            run_ref[...] = run

    def join_maps(before, after):
        both = dot3(after[:, :, :DK], before, 2, 1, 1)
        return jnp.concatenate([both[:, :, :DK], both[:, :, DK:] + after[:, :, DK:]], 2)

    mine_at = core * each if halved else 0
    theirs_at = (1 - core) * each if halved else 0

    def give(which):
        at = pl.ds(theirs_at if which == 0 else mine_at, each)
        return remote(
            sent_map.at[at], sib_map.at[at], pair_send.at[which], pair_recv.at[which], (sibling, z)
        )

    def taken(which):
        at = pl.ds(mine_at if which == 0 else theirs_at, each)
        return remote(
            sent_map.at[at], sib_map.at[at], pair_send.at[which], pair_recv.at[which], (sibling, z)
        )

    def give_rest(act):
        if halved:

            @pl.when(core == 0)
            def _():
                act(give(1))

    def to_chip(n, source, dest):
        src, dst = total.at[n], got.at[source, n]
        if source == 0:
            src, dst = total.at[n, :, pl.ds(DK, DV)], got.at[0, n, :, pl.ds(DK, DV)]
        return remote(
            src, dst, chip_send.at[dest, n], chip_recv.at[source, n], (dest * 2 + core, z)
        )

    def back(n, start):
        here = prev.at[start + n]
        return remote(here, here, back_send.at[n], back_recv.at[n], (sibling, z))

    for n in range(streams):
        process(n)
        if n < 2 < streams:
            token_step(2, quarter(2 * n))
        if n < streams - 1:
            reads(n)
        if n < 2 < streams:
            token_step(2, quarter(2 * n + 1))
        elif 2 <= n < streams - 1:
            token_step(n + 1, range(PIECES))

    def carries():
        for c in range(1, streams - 1):
            step_ref[c] = join_maps(step_ref[c - 1], step_ref[c])

    def join():
        taken(0).wait_recv()

        @pl.when(chip < chips - 1)
        def _():
            at = pl.ds(mine_at, each)
            own = run_ref[at]
            other = sib_map[at].astype(F32)
            before = jnp.where(core == 0, own, other)
            after = jnp.where(core == 0, other, own)
            total[...] = join_maps(before, after).astype(BF16)

        for source in range(chips - 1):

            @pl.when(chip == source)
            def _():
                for n in range(each):
                    for dest in range(chips - 1, source, -1):
                        to_chip(n, source, dest).start()

    def prefixes():
        for c in range(1, streams):
            both = dot3(query_ref[:, c], step_ref[c - 1], 2, 1, 1)
            query_ref[:, c] = both[:, :, :DK]
            read_ref[:, c] = read_ref[:, c] + both[:, :, DK:]

    def enter(n):
        h = mine_at + n

        @pl.when(chip == 0)
        def _():
            prev[h] = jnp.zeros((DK, DV), F32)

        for source in range(chips - 1):

            @pl.when(chip > source)
            def _():
                to_chip(n, source, chip).wait_recv()
                if source == 0:
                    prev[h] = got[0, n, :, DK:].astype(F32)
                else:
                    prev[h] = dot2(got[source, n, :, :DK], prev[h]) + got[
                        source, n, :, DK:
                    ].astype(F32)

        if halved:

            @pl.when(chip > 0)
            def _():
                back(n, mine_at).start()

    def hear(n):
        h = theirs_at + n

        @pl.when(chip == 0)
        def _():
            prev[h] = jnp.zeros((DK, DV), F32)

        @pl.when(chip > 0)
        def _():
            back(n, theirs_at).wait_recv()

    def spot(h, source):
        at = pl.multiple_of((source * heads + h) * DV, DV)
        return out_ref.at[:, pl.ds(at, DV)]

    def outgoing(h, n):
        dest = partner(n)
        return remote(
            mixed.at[h, dest], spot(h, z), out_send.at[0], out_recv.at[z], (t, dest)
        )

    def own_out(h):
        return pltpu.make_async_copy(mixed.at[h, z], spot(h, z), out_own.at[0])

    far = list(reversed(near))

    def finish(h):
        carried = prev[h]
        state[...] = carried

        @pl.when(core == 1)
        def _():
            state[...] = dot2(sib_map[h, :, :DK], carried) + sib_map[h, :, DK:].astype(F32)

        reads = dot3(query_ref[h].reshape(streams * local, DK), state[...], 1, 0)
        read = read_ref[h].reshape(streams * local, DV) + reads
        readout = read.astype(BF16).astype(F32)
        scale = lax.rsqrt(jnp.mean(readout * readout, -1, keepdims=True) + 1e-06)
        mixed[h] = (readout * scale * gain_ref[...]).astype(BF16).reshape(streams, local, DV)
        for n in reversed(ranks):
            outgoing(h, n).start()
        own_out(h).start()

    join()
    reads(streams - 1)
    carries()
    prefixes()
    for n in range(each):
        enter(n)
        finish(mine_at + n)
    if halved:

        @pl.when(core == 1)
        def _():
            taken(1).wait_recv()

        for n in range(each):
            hear(n)
            finish(theirs_at + n)

    drain(mixed.at[:, 0], out_own.at[0])
    for i in far:
        drain(mixed.at[:, 0], out_recv.at[lax.rem(z + i, streams)])
    drain(mixed.at[:, pl.ds(0, streams - 1)], out_send.at[0])
    give(0).wait_send()
    give_rest(lambda copy: copy.wait_send())
    for n in range(each):
        for source in range(chips - 1):

            @pl.when(chip == source)
            def _():
                for dest in range(chips - 1, source, -1):
                    to_chip(n, source, dest).wait_send()

        if halved:

            @pl.when(chip > 0)
            def _():
                back(n, mine_at).wait_send()

    def sent():
        drain(stage.at[pl.ds(0, streams - 1)], cross_send.at[0])
        for i in range(1, chips):
            drain(full.at[pl.ds(0, streams - 1), pl.ds(0, share)], plane_send.at[i])

    only(is_sender, sent)
    if paired:
        drain(full.at[pl.ds(0, streams - 1), pl.ds(0, origins * share)], pass_send.at[0])
    else:

        @pl.when(core == 0)
        def _():
            drain(full.at[pl.ds(0, streams - 1), pl.ds(0, origins * share)], pass_send.at[0])

    drain(gates.at[0, pl.ds(0, streams - 1)], gate_send.at[0])
    drain(gates.at[0, pl.ds(0, streams - 1)], gate_pass.at[0])

    def whole_of(k):
        return local - part * len(direct) if k == streams - 2 else local

    if len(direct) > 0:

        @pl.when((z == 0) | (z == streams - 1))
        def _():
            drain(x_ref.at[z, pl.ds(0, part * len(direct))], across_send.at[0])

    for k in range(streams):

        @pl.when((z >= k) & (z < streams - 1))
        def _():
            drain(x_ref.at[z - k, pl.ds(0, whole_of(k))], right_sem.at[z - k])

        @pl.when((z + k < streams) & (z > 0))
        def _():
            drain(x_ref.at[z + k, pl.ds(0, whole_of(k))], left_sem.at[z + k])


def shards(
    tokens, w_query, w_key, w_value, decay_proj, beta_proj, decay_rate, beta_bias, norm_gain
):
    streams = lax.axis_size("stream")
    places = lax.axis_size("tm")
    heads = HEADS // streams
    depth = w_query.shape[0]
    senders = min(places, depth // 16)
    share = depth // senders
    local, features = tokens.shape
    chips = places // 2
    width = 3 * heads * DK
    each = heads // 2 if heads % 2 == 0 else heads
    any_space = pl.BlockSpec(memory_space=pl.ANY)
    vmem = pl.BlockSpec(memory_space=pltpu.VMEM)
    dma = pltpu.SemaphoreType.DMA
    return pl.pallas_call(
        functools.partial(layer_kernel, streams, places, heads, senders),
        out_shape=pltpu.VMEM((local, HEADS * DV), BF16),
        in_specs=[any_space] * 6 + [vmem] * 3,
        out_specs=vmem,
        scratch_shapes=[
            pltpu.VMEM((streams, local, features), BF16),
            pltpu.VMEM((streams, depth, width), BF16),
            pltpu.VMEM((streams, share, width), BF16),
            pltpu.VMEM((2, streams, HEADS, depth), BF16),
            pltpu.VMEM((HEADS, CHUNK), F32),
            pltpu.VMEM((heads, CHUNK, DK), BF16),
            pltpu.VMEM((heads, CHUNK, CHUNK), F32),
            pltpu.VMEM((heads, CHUNK, DK), F32),
            pltpu.VMEM((heads, CHUNK, DK + DV), F32),
            pltpu.VMEM((streams, heads, DK, DK + DV), F32),
            pltpu.VMEM((heads, DK, DK + DV), F32),
            pltpu.VMEM((heads, streams, CHUNK, DV), F32),
            pltpu.VMEM((heads, streams, CHUNK, DK), F32),
            pltpu.VMEM((heads, DK, DK + DV), BF16),
            pltpu.VMEM((heads, DK, DK + DV), BF16),
            pltpu.VMEM((each, DK, DK + DV), BF16),
            pltpu.VMEM((chips, each, DK, DK + DV), BF16),
            pltpu.VMEM((heads, DK, DV), F32),
            pltpu.VMEM((DK, DV), F32),
            pltpu.VMEM((heads, streams, local, DV), BF16),
            dma((streams,)),
            dma((1,)),
            dma((1,)),
            dma((1,)),
            dma((1,)),
            dma((streams,)),
            dma((1,)),
            dma((1,)),
            dma((streams,)),
            dma((streams,)),
            dma((1,)),
            dma((streams, PIECES)),
            dma((1,)),
            dma((streams,)),
            dma((chips,)),
            dma((senders // 2 if senders == places else senders, streams)),
            dma((1,)),
            dma((1,)),
            dma((2,)),
            dma((2,)),
            dma((chips, each)),
            dma((chips, each)),
            dma((each,)),
            dma((each,)),
            dma((1,)),
            dma((streams,)),
            dma((1,)),
        ],
        compiler_params=pltpu.CompilerParams(collective_id=0, has_side_effects=True),
    )(
        tokens,
        w_query,
        w_key,
        w_value,
        decay_proj.T,
        beta_proj.T,
        decay_rate[None],
        beta_bias[None],
        norm_gain[None],
    )


def solution(mesh):
    return jax.shard_map(
        shards,
        mesh=mesh,
        in_specs=(
            P(("tm", "stream"), None),
            P("stream", None),
            P("stream", None),
            P("stream", None),
            P("stream", None),
            P("stream", None),
            P(),
            P(),
            P(),
        ),
        out_specs=P(("tm", "stream"), None),
        check_vma=False,
    )
```
